32 devices in a mesh: parts: 2 (over y), seq: 4 (over z), head: 4 (over x, core).
Axes of the slice: x: 2, y: 2, z: 4, core: 2. Of those that a mesh axis runs over, the one named last changes fastest.
Arguments:
- xs: bfloat16 [8192, 5120], P(('parts', 'seq'), 'head'), parts along dimension 0, may hold values from -70 to 70
- gate_in: bfloat16 [8192, 5120], P(('parts', 'seq'), 'head'), parts along dimension 0, may hold values from -6 to 6
- bc_in: bfloat16 [8192, 256], P(('parts', 'seq')), parts along dimension 0, may hold values from -6 to 6
- dt_in: bfloat16 [8192, 64], P(('parts', 'seq'), 'head'), parts along dimension 0, may hold values from -3 to 3
- placement: int32 [8192], P(('parts', 'seq')), parts along dimension 0, may hold values from 0 to 4095, as said below
- lengths: int32 [6], P('parts'), parts along dimension 0, may hold values from 1 to 3072, 4096 in all
- conv_x: float32 [4, 5120], P(None, 'head'), may hold values from -3 to 3
- conv_bc: float32 [4, 256], replicated, may hold values from -3 to 3
- a_log: float32 [64], P('head'), may hold values from -9.5 to -0.5
- dt_bias: float32 [64], P('head'), may hold values from -3 to -1
- d_skip: float32 [64], P('head'), may hold values from 0.3 to 3
- norm_gain: float32 [5120], P('head'), may hold values from 0.1 to 1.9
Outputs:
- mixed: bfloat16 [8192, 5120], P(('parts', 'seq'), 'head'), parts along dimension 0
The draws below stay inside these ranges and needn't reach their ends.
There are 2 independent parts, one for each index of `parts`. The reference program is written for one: setup_inputs(seed, part) draws one part's arguments, and reference() takes and returns one part's arrays. A program takes and returns all parts, laid end to end along the dimension named above; an argument that names none is the same for every part. Nothing has to cross between parts.
Inputs may be any that keep to these rules, and one draw needn't show every extreme that they name: `placement`: A permutation of the packed positions; each ingest device holds exactly 1024 // 4 rows bound for every sequence shard. The lengths sum to 4096; the longest is 3072.
All inputs are finite; a program needn't handle non-finite values.
Results may differ from the reference program's by a relative error of at most 0.0025.
The reference program's roundings to bfloat16 on the way (of `convolved`) count: a program that leaves them out, or rounds other values in their place, can miss the bound.
Values may be sent and summed in bfloat16 or wider, within the bound.
A program may use at most 128 MiB of HBM per device.

```python
import math
import jax
import jax.numpy as jnp
import numpy as np
from jax import lax

HEADS = 64
HEAD_DIM = 80
STATE = 128
KCONV = 4
BLOCK = 256
SEQS = 3
TOK_DEV = 1024
INNER = 5120
TOKENS = 4096


def draw_placement(key, part):
    shard_count = TOKENS // TOK_DEV
    share = TOK_DEV // shard_count
    first_keys = jax.random.split(jax.random.fold_in(key, 11), shard_count)
    orders = jax.vmap(lambda single: jax.random.permutation(single, TOK_DEV))(first_keys)
    slots = orders.astype(jnp.int32) + (jnp.arange(shard_count, dtype=jnp.int32) * TOK_DEV)[:, None]
    slots = slots.reshape(shard_count, shard_count, share).transpose(1, 0, 2).reshape(shard_count, TOK_DEV)
    second_keys = jax.random.split(jax.random.fold_in(key, 12), shard_count)
    shuffles = jax.vmap(lambda single: jax.random.permutation(single, TOK_DEV))(second_keys)
    slots = jnp.take_along_axis(slots, shuffles.astype(jnp.int32), axis=1)
    return slots.reshape(-1).astype(jnp.int32)


def draw_xs(key, part):
    columns = jnp.arange(INNER, dtype=jnp.float32) / INNER
    scales = 0.5 * jnp.power(10.0, columns)
    values = jnp.clip(jax.random.normal(key, (TOKENS, INNER), jnp.float32), -6.0, 6.0)
    return (values * scales[None, :]).astype(jnp.bfloat16)


def draw_a_log(key, part):
    return jax.random.uniform(key, (HEADS,), jnp.float32, -9.5, -0.5)


def level_of(rng, dims, cuts, least, largest):
    loudness, own = 1.0, jax.random.fold_in(rng, 6)
    for dim, shards_of in cuts:
        draws = jnp.exp(jax.random.uniform(jax.random.fold_in(own, dim), (shards_of,), jnp.float32, least / len(cuts), largest / len(cuts)))
        loudness = loudness * jnp.repeat(draws, dims[dim] // shards_of).reshape([-1 if axis == dim else 1 for axis in range(len(dims))])
    return loudness


def profile(amount, total, reach, slope):
    weights = [(1 << 20) // math.isqrt(grade ** slope) + 1 for grade in range(2, amount + 1)]
    rest, counts = total - reach - (amount - 1), [1] * (amount - 1)
    while rest > 0:
        movable = [i for i in range(amount - 1) if counts[i] < reach]
        whole, remaining = sum([weights[i] for i in movable]), rest
        for i in movable:
            extra = min(reach - counts[i], max(1, remaining * weights[i] // whole), rest)
            counts[i] = counts[i] + extra
            rest = rest - extra
    return np.array([reach] + counts)


def ragged(key, number_of, total, limit, slope):
    if number_of == 2:
        one = jax.random.randint(key, (), max(1, total - limit), min(limit, total - 1) + 1)
        return jnp.stack([one, total - one])
    sizes = jnp.asarray(profile(number_of, total, limit, slope), jnp.int32)
    twos = (number_of - 1) // 2
    giver, taker = sizes[1:1 + 2 * twos:2], sizes[2:2 + 2 * twos:2]
    margin = jnp.minimum(giver - 1, limit - taker)
    passed = jax.random.randint(jax.random.fold_in(key, 1), (twos,), 0, 1 << 20) % (margin + 1)
    sizes = sizes.at[1:1 + 2 * twos:2].set(giver - passed).at[2:2 + 2 * twos:2].set(taker + passed)
    return sizes[jax.random.permutation(jax.random.fold_in(key, 2), number_of)]


def centred(own_key, dims, scale, bound, shards=(), held_as=jnp.bfloat16):
    values = jax.random.normal(own_key, dims, jnp.float32) * scale
    if len(shards) > 0:
        values = level_of(own_key, dims, shards, -0.22, 0.18) * values
    return jnp.clip(values, min=-bound, max=bound).astype(held_as)


def setup_inputs(seed: int = 0, part: int = 0) -> dict:
    arg_keys = jax.random.split(jax.random.key(seed), 13)
    part_splits = jax.random.split(jax.random.fold_in(arg_keys[12], part), 13)
    return {
        "xs": draw_xs(jax.random.fold_in(jax.random.fold_in(arg_keys[12], part), 71), part),
        "gate_in": centred(part_splits[1], (TOKENS, INNER), 1.0, 6.0, ((0, 4), (1, 4))),
        "bc_in": centred(part_splits[2], (TOKENS, 2 * STATE), 1.0, 6.0, ((0, 4),)),
        "dt_in": centred(part_splits[3], (TOKENS, HEADS), 0.5, 3.0, ((0, 4), (1, 4))),
        "placement": draw_placement(jax.random.fold_in(jax.random.fold_in(arg_keys[12], part), 71), part),
        "lengths": ragged(part_splits[5], SEQS, TOKENS, 3 * TOKENS // 4, 2).astype(jnp.int32),
        "conv_x": centred(arg_keys[6], (KCONV, INNER), 0.5, 3.0, ((1, 4),), jnp.float32),
        "conv_bc": centred(arg_keys[7], (KCONV, 2 * STATE), 0.5, 3.0, (), jnp.float32),
        "a_log": draw_a_log(jax.random.fold_in(arg_keys[12], 71), part),
        "dt_bias": jnp.clip(-3.0 + 2.0 * jax.random.uniform(arg_keys[9], (HEADS,), jnp.float32) ** level_of(arg_keys[9], (HEADS,), ((0, 4),), -0.2, 0.2), -3.0, -1.0),
        "d_skip": jnp.clip(jnp.exp(math.log(3.0) - 2.3025851 * jax.random.uniform(arg_keys[10], (HEADS,), jnp.float32) ** level_of(arg_keys[10], (HEADS,), ((0, 4),), -0.2, 0.2)), 0.3, 3.0),
        "norm_gain": jnp.clip(1.0 + 0.18 * jax.random.normal(arg_keys[11], (INNER,), jnp.float32), 0.1, 1.9),
    }


highest = lax.Precision.HIGHEST

def convolve(rows, docs_rows, kernel):
    width = kernel.shape[0]
    count = rows.shape[0] - (width - 1)
    total = jnp.zeros((count, rows.shape[1]), jnp.float32)
    for lag in range(width):
        lower = width - 1 - lag
        match = (docs_rows[lower:lower + count] == docs_rows[width - 1:]).astype(jnp.float32)
        total = total + kernel[lag][None, :] * rows[lower:lower + count].astype(jnp.float32) * match[:, None]
    return jax.nn.silu(total).astype(jnp.bfloat16)

def block_pass(carry_state, pieces):
    conv_rows, key_rows, query_rows, step_sizes, log_decay, begins = pieces
    length = step_sizes.shape[0]
    head_count = step_sizes.shape[1]
    log_sums = jnp.cumsum(log_decay, axis=0)
    resets = jnp.cumsum(begins)
    places = jnp.arange(length)
    linked = (places[:, None] >= places[None, :]) & (resets[:, None] == resets[None, :])
    log_gaps = log_sums[:, None, :] - log_sums[None, :, :]
    weights = jnp.exp(jnp.where(linked[:, :, None], log_gaps, -jnp.inf))
    scores = jnp.dot(query_rows, key_rows.T, preferred_element_type=jnp.float32)
    mixing = scores[:, :, None] * weights * step_sizes[None, :, :]
    inputs = conv_rows.astype(jnp.float32).reshape(length, head_count, -1)
    outputs = jnp.einsum('tsh,shp->thp', mixing, inputs, precision=highest)
    carried = jnp.where((resets == 0)[:, None], jnp.exp(log_sums), 0.0)
    queries = query_rows.astype(jnp.float32)
    outputs = outputs + carried[:, :, None] * jnp.einsum('tn,hpn->thp', queries, carry_state, precision=highest)
    closing = jnp.where((resets == resets[-1])[:, None], jnp.exp(log_sums[-1][None, :] - log_sums), 0.0) * step_sizes
    key_values = key_rows.astype(jnp.float32)
    carry_state = carried[-1][:, None, None] * carry_state + jnp.einsum('sh,shp,sn->hpn', closing, inputs, key_values, precision=highest)
    return (carry_state, outputs.reshape(length, -1))

def reference(xs, gate_in, bc_in, dt_in, placement, lengths, conv_x, conv_bc, a_log, dt_bias, d_skip, norm_gain):
    packed_x = jnp.zeros_like(xs).at[placement].set(xs)
    packed_gate = jnp.zeros_like(gate_in).at[placement].set(gate_in)
    packed_bc = jnp.zeros_like(bc_in).at[placement].set(bc_in)
    packed_dt = jnp.zeros_like(dt_in).at[placement].set(dt_in)
    starts = (jnp.cumsum(lengths) - lengths).astype(jnp.int32)
    positions = jnp.arange(TOKENS + KCONV - 1, dtype=jnp.int32) - (KCONV - 1)
    docs = lax.optimization_barrier(jnp.sum((starts[None, :] <= positions[:, None]).astype(jnp.int32), axis=1)) - 1
    begin_all = lax.optimization_barrier(jnp.sum((starts[None, :] == positions[KCONV - 1:, None]).astype(jnp.int32), axis=1))
    channels = jnp.concatenate([packed_x, packed_bc], 1)
    padded = jnp.concatenate([jnp.zeros((KCONV - 1, channels.shape[1]), channels.dtype), channels], 0)
    kernel = jnp.concatenate([conv_x, conv_bc], 1)
    step_all = jax.nn.softplus(packed_dt.astype(jnp.float32) + dt_bias[None, :])
    decay_all = -jnp.exp(a_log)[None, :] * step_all

    def one_block(carry_state, block):
        first = (block * BLOCK).astype(jnp.int32)
        rows = lax.dynamic_slice_in_dim(padded, first, BLOCK + KCONV - 1, 0)
        docs_rows = lax.dynamic_slice_in_dim(docs, first, BLOCK + KCONV - 1, 0)
        convolved = convolve(rows, docs_rows, kernel)
        conv_rows = convolved[:, :INNER]
        key_rows = convolved[:, INNER:INNER + STATE]
        query_rows = convolved[:, INNER + STATE:]
        step_sizes = lax.dynamic_slice_in_dim(step_all, first, BLOCK, 0)
        log_decay = lax.dynamic_slice_in_dim(decay_all, first, BLOCK, 0)
        begins = lax.dynamic_slice_in_dim(begin_all, first, BLOCK, 0)
        carry_state, outputs = block_pass(carry_state, (conv_rows, key_rows, query_rows, step_sizes, log_decay, begins))
        inputs = conv_rows.astype(jnp.float32).reshape(BLOCK, HEADS, HEAD_DIM)
        outputs = outputs + (d_skip[None, :, None] * inputs).reshape(BLOCK, INNER)
        gates = lax.dynamic_slice_in_dim(packed_gate, first, BLOCK, 0)
        gated = outputs * jax.nn.silu(gates.astype(jnp.float32))
        mean_square = lax.optimization_barrier(jnp.sum(gated * gated, axis=1)) / INNER
        result = gated * lax.rsqrt(mean_square + 1e-05)[:, None] * norm_gain[None, :]
        return (carry_state, result.astype(jnp.bfloat16))
    empty = jnp.zeros((HEADS, HEAD_DIM, STATE), jnp.float32)
    blocks = jnp.arange(TOKENS // BLOCK, dtype=jnp.int32)
    final_state, results = lax.scan(one_block, empty, blocks)
    return results.reshape(TOKENS, INNER)
```

```python
import functools

import jax
import jax.numpy as jnp
from jax import lax
from jax.experimental import pallas as pl
from jax.experimental.pallas import tpu as pltpu
from jax.sharding import PartitionSpec as P

BLOCK = 256
LANES = 128
RIM = 8
GROUPS = 2
WINDOW = 2
BAND = 16
TAIL = 48
HIGHEST = lax.Precision.HIGHEST
MESH = pl.DeviceIdType.MESH
F32 = jnp.float32
BF16 = jnp.bfloat16


def iota(shape, dim):
    return lax.broadcasted_iota(jnp.int32, shape, dim)


def dot(a, b, dims=((1,), (0,))):
    return lax.dot_general(a, b, (dims, ((), ())), preferred_element_type=F32)


def halves(value):
    high = value.astype(BF16)
    return high, (value - high.astype(F32)).astype(BF16)


def dot_left(a, b):
    high, low = halves(a)
    return dot(high, b) + dot(low, b)


def dot_right(a, b):
    high, low = halves(b)
    return dot(jnp.concatenate([a, a], 1), jnp.concatenate([high, low], 0))


def dot_turned(a, b):
    high, low = halves(b)
    dims = ((0,), (0,))
    return dot(a, high, dims) + dot(a, low, dims)


def remote(source, target, sends, receives, axis, offset):
    count, me = lax.axis_size(axis), lax.axis_index(axis)
    return pltpu.make_async_remote_copy(
        src_ref=source,
        dst_ref=target,
        send_sem=sends,
        recv_sem=receives,
        device_id={axis: lax.rem(me + offset, count)},
        device_id_type=MESH,
    )


def each(first, last, action):
    def once(i, _):
        action(i)
        return 0

    lax.fori_loop(first, last, once, 0)


def doc_at(starts, position):
    total = jnp.where(starts[0] <= position, 1, 0)
    for start in starts[1:]:
        total = total + jnp.where(start <= position, 1, 0)
    return total


def starts_of(length_ref):
    starts = [jnp.int32(0)]
    for j in range(length_ref.shape[0] - 1):
        starts.append(starts[-1] + length_ref[j])
    return starts


def head_row(ref):
    lane = iota((8, LANES), 1)
    row = jnp.zeros((8, LANES), F32)
    for head in range(ref.shape[0]):
        row = jnp.where(lane == head, ref[head], row)
    return row


def expanded(value, inside):
    high, low = halves(value)
    low = pltpu.roll(low.astype(F32), LANES // 2, 1)
    lane = iota((1, LANES), 1)
    both = jnp.where(lane < LANES // 2, high.astype(F32), low)
    return dot(both.astype(BF16), inside)


def block_of(chunk, size=BLOCK):
    if isinstance(chunk, int):
        return pl.ds(chunk * size, size)
    return pl.ds(pl.multiple_of(chunk * size, size), size)


def one_hot(keys, first, count):
    return (iota((count, keys.shape[1]), 0) + first == keys).astype(F32).astype(BF16)


def slots_of(target, groups):
    rows = target.shape[1]
    chosen = (iota((groups, rows), 0) == target).astype(F32)
    before = (iota((LANES, LANES), 0) < iota((LANES, LANES), 1)).astype(F32).astype(BF16)
    blocks = [chosen[:, k : k + LANES] for k in range(0, rows, LANES)]
    inside = dot(jnp.concatenate(blocks, 0).astype(BF16), before)
    offset = jnp.zeros((groups, 1), F32)
    slots = []
    for k, block in enumerate(blocks):
        ranks = inside[k * groups : (k + 1) * groups, :] + offset
        slots.append(jnp.sum(block * ranks, axis=0, keepdims=True))
        offset = offset + jnp.sum(block, axis=1, keepdims=True)
    return jnp.concatenate(slots, 1).astype(jnp.int32)


def layer_kernel(
    heads, length_ref, a_log_ref, dt_bias_ref, d_skip_ref, place_ref, dt_ref, conv_x_ref, conv_bc_ref,
    x_hbm, gate_hbm, bc_hbm,
    y_hbm, total_ref,
    given, bc_ref, sort_ref, unsort_ref, send, came, small_send, small_in, small_all,
    bc_send, bc_all, rim_rows, rim_send, rim_in, rim_ref, packed_ref, avail_ref, inside_ref,
    x_ref, key_ref, query_ref, y_ref, sums_ref, sums_t_ref, step_t_ref, scores_ref,
    carried_ref, closing_ref, carry_ref, before_ref, state_ref, state_in, state_out, skip_ref,
    square_ref, squares,
    load_sems, sems, small_sems, bc_sems, rim_sems, wide_sems, state_sems, square_sems, store_sems,
):
    shards, peers = lax.axis_size("seq"), lax.axis_size("head")
    me, own = lax.axis_index("seq"), lax.axis_index("head")
    rows, inner = y_ref.shape
    per = rows // shards
    half = per // (peers // 2)
    head_dim = inner // heads
    chunks = rows // BLOCK
    pieces = inner // LANES
    wide = 2 * LANES
    pairs = pieces // 2
    width = conv_x_ref.shape[0]
    group_heads = heads // GROUPS
    span = inner // GROUPS
    group_pieces = pieces // GROUPS
    base = me * rows
    mine = pl.ds(pl.multiple_of(me * per, per), per)
    starts = starts_of(length_ref)

    def load(pair):
        source = x_hbm if pair < pairs else gate_hbm
        first = (pair if pair < pairs else pair - pairs) * wide
        return pltpu.make_async_copy(source.at[:, first : first + wide], given.at[pair], load_sems.at[pair])

    bc_load = pltpu.make_async_copy(bc_hbm, bc_ref, load_sems.at[2 * pairs])

    def part(owner):
        return pl.ds(pl.multiple_of(owner * per, per), per)

    def piece_copy(q, i):
        return remote(
            send.at[q, part(lax.rem(me + i, shards))], came.at[q, mine],
            sems.at[0, q, i], sems.at[1, q, i], "seq", i,
        )

    def small_copy(i):
        return remote(
            small_send.at[lax.rem(me + i, shards)], small_in.at[me],
            small_sems.at[0, i], small_sems.at[1, i], "seq", i,
        )

    def bc_copy(i):
        dest = lax.rem(me + i, shards)
        return remote(
            bc_send.at[pl.ds(pl.multiple_of(dest * half, half), half)],
            bc_all.at[own, pl.ds(pl.multiple_of(me * half, half), half)],
            bc_sems.at[0, i], bc_sems.at[1, i], "seq", i,
        )

    def rim_copy(i):
        return remote(
            rim_send.at[lax.rem(me + i, shards)], rim_in.at[me],
            rim_sems.at[0, i], rim_sems.at[1, i], "seq", i,
        )

    def wide_copy(i):
        return remote(bc_all.at[own], bc_all.at[own], wide_sems.at[0, i], wide_sems.at[1, i], "head", i)

    def state_copy(group):
        return remote(
            state_out.at[group], state_in.at[group],
            state_sems.at[0, group], state_sems.at[1, group], "seq", 1,
        )

    def square_copy(i):
        return remote(
            squares.at[own], squares.at[own], square_sems.at[0, i], square_sems.at[1, i], "head", i
        )

    def store(j):
        cols = slice(j * LANES, (j + 1) * LANES) if isinstance(j, int) else pl.ds(
            pl.multiple_of(j * LANES, LANES), LANES
        )
        return pltpu.make_async_copy(y_ref.at[:, cols], y_hbm.at[:, cols], store_sems.at[j])

    def start(q):
        each(1, shards, lambda i: piece_copy(q, i).start())

    def receive(q):
        each(1, shards, lambda i: piece_copy(q, i).wait_recv())

    for pair in range(2 * pairs):
        load(pair).start()
        if pair == 0:
            bc_load.start()
    barrier = pltpu.get_barrier_semaphore()
    for axis in ("seq", "head"):
        count, here = lax.axis_size(axis), lax.axis_index(axis)

        def signal(i, axis=axis, count=count, here=here):
            pl.semaphore_signal(
                barrier, inc=1, device_id={axis: lax.rem(here + i, count)}, device_id_type=MESH
            )

        each(1, count, signal)

    place = place_ref[0:1, :]
    target = lax.shift_right_logical(place, rows.bit_length() - 1)
    local = place & (rows - 1)
    slot = slots_of(target, -(-shards // 16) * 16)
    key = target * per + slot

    def sort_rows(b):
        sort_ref[block_of(b), :] = one_hot(key, b * BLOCK, BLOCK)

    each(0, chunks, sort_rows)

    def pick(pair):
        def rows_of(b):
            value = dot(sort_ref[block_of(b), :], given[pair]).astype(BF16)
            send[2 * pair, block_of(b), :] = value[:, :LANES]
            send[2 * pair + 1, block_of(b), :] = value[:, LANES:]

        each(0, chunks, rows_of)
        for q in (2 * pair, 2 * pair + 1):
            came[q, mine, :] = send[q, mine, :]

    digits = jnp.concatenate(
        [
            dt_ref[...],
            jnp.where(
                iota((16, rows), 0) == 0, local >> 5, jnp.where(iota((16, rows), 0) == 1, local & 31, 0)
            ).astype(F32).astype(BF16),
        ],
        0,
    )

    def small_rows(d):
        small_send[d] = dot(digits, sort_ref[part(d), :], ((1,), (1,))).astype(BF16)

    each(0, shards, small_rows)
    small_in[me] = small_send[me]
    load(0).wait()
    pick(0)
    bc_load.wait()
    bc_cols = pl.ds(pl.multiple_of(lax.rem(own, 2) * LANES, LANES), LANES)
    bc_first = own // 2 * half

    def bc_rows(d):
        source = sort_ref[pl.ds(pl.multiple_of(d * per + bc_first, half), half), :]
        bc_send[pl.ds(pl.multiple_of(d * half, half), half), :] = dot(source, bc_ref[:, bc_cols]).astype(BF16)

    each(0, shards, bc_rows)
    bc_mine = pl.ds(pl.multiple_of(me * half, half), half)
    bc_all[own, bc_mine, :] = bc_send[bc_mine, :]

    pl.semaphore_wait(barrier, shards - 1 + peers - 1)
    each(1, shards, lambda i: small_copy(i).start())
    each(1, shards, lambda i: bc_copy(i).start())
    start(0)

    line = iota((RIM * shards, 1), 0)
    back = line & (RIM - 1)
    wanted = lax.shift_right_logical(line, RIM.bit_length() - 1) * rows - (width - 1) + back
    wanted = jnp.where((back < width - 1) & (wanted >= 0), wanted, -1)
    rim_pick = (wanted == place).astype(F32).astype(BF16)
    rim_rows[...] = jnp.zeros_like(rim_rows)

    def rim_put(value, j):
        for d in range(shards):
            for k in range(width - 1):
                rim_rows[d, pl.ds(k * BAND + j, 1), :] = value[d * RIM + k : d * RIM + k + 1, :]

    def rim_of(value, j):
        rim_put(value[:, :LANES], j)
        rim_put(value[:, LANES:], j + 1)

    rim_of(dot(rim_pick, bc_ref[...]), pieces)
    for pair in range(1, pairs):
        load(pair).wait()
    each(0, pairs, lambda pair: rim_of(dot(rim_pick, given[pair]), 2 * pair))
    rim_send[...] = rim_rows[...].astype(BF16)
    rim_in[me] = rim_send[me]
    each(1, shards, lambda i: rim_copy(i).start())
    start(1)
    each(1, pairs, pick)

    for b in range(chunks):
        position = iota((BLOCK, 1), 0) + (base + b * BLOCK)
        first = jnp.zeros((BLOCK, 1), jnp.int32)
        for begin in starts[1:]:
            first = jnp.where(begin <= position, begin, first)
        avail_ref[b * BLOCK : (b + 1) * BLOCK, :] = jnp.broadcast_to(position - first, (BLOCK, LANES))
    head, channel = iota((LANES, inner), 0), iota((LANES, inner), 1)
    head = jnp.where(head < LANES // 2, head, head - LANES // 2)
    inside = (channel >= head * head_dim) & (channel < (head + 1) * head_dim)
    inside_ref[...] = inside.astype(F32).astype(BF16)
    skip_ref[...] = expanded(head_row(d_skip_ref), inside_ref[...])
    state_ref[...] = jnp.zeros_like(state_ref)
    before_ref[...] = jnp.zeros_like(before_ref)
    square_ref[...] = jnp.zeros_like(square_ref)
    small_all[...] = jnp.zeros_like(small_all)

    each(1, shards, lambda i: bc_copy(i).wait())
    each(1, peers, lambda i: wide_copy(i).start())
    each(1, shards, lambda i: small_copy(i).wait())
    lines = small_in.shape[1]
    if per % LANES == 0:
        for s in range(shards):
            small_all[0:lines, s * per : (s + 1) * per] = small_in[s]
    else:
        total = jnp.zeros((lines, rows), F32)
        for s in range(shards):
            spread = (iota((per, rows), 0) + s * per == iota((per, rows), 1)).astype(F32).astype(BF16)
            total = total + dot(small_in[s], spread)
        small_all[0:lines, :] = total.astype(BF16)
    high = small_all[heads : heads + 1, :].astype(F32)
    low = small_all[heads + 1 : heads + 2, :].astype(F32)
    landed = (high * 32.0 + low).astype(jnp.int32)

    def unsort_rows(b):
        unsort_ref[block_of(b), :] = one_hot(landed, b * BLOCK, BLOCK)

    each(0, chunks, unsort_rows)

    def convolve(value, j, taps_ref, col, out_ref):
        packed_ref[RIM:, :] = value
        for k in range(width - 1):
            packed_ref[RIM - (width - 1) + k : RIM - (width - 1) + k + 1, :] = rim_ref[pl.ds(k * BAND + j, 1), :]
        taps = taps_ref[:, col]
        total = taps[0:1, :] * packed_ref[RIM:, :]
        for lag in range(1, width):
            moved = taps[lag : lag + 1, :] * packed_ref[RIM - lag : RIM - lag + rows, :]
            total = total + jnp.where(avail_ref[...] >= lag, moved, 0.0)
        out_ref[:, col] = (total * jax.nn.sigmoid(total)).astype(BF16)

    def x_piece(j):
        col = pl.ds(pl.multiple_of(j * LANES, LANES), LANES)
        convolve(dot(unsort_ref[...], came[j]), j, conv_x_ref, col, x_ref)

    def pump(q):
        receive(q)
        if isinstance(q, int):
            if q + WINDOW < 2 * pieces:
                start(q + WINDOW)
        else:

            @pl.when(q + WINDOW < 2 * pieces)
            def _():
                start(q + WINDOW)

    for pair in range(pairs, 2 * pairs):
        load(pair).wait()
    def project():
        for side in range(2):
            quarters = [bc_all[2 * r + side].reshape(shards, half, LANES) for r in range(peers // 2)]
            together = jnp.concatenate(quarters, 1).reshape(rows, LANES)
            value = dot(unsort_ref[...], together)
            here = slice(side * LANES, (side + 1) * LANES)
            if side == 0:
                convolve(value, pieces, conv_bc_ref, here, key_ref)
            else:
                convolve(value, pieces + 1, conv_bc_ref, here, query_ref)

    def common(chunk):
        origin = base + chunk * BLOCK
        here = block_of(chunk)
        column = iota((BLOCK, 1), 0) + origin
        document = doc_at(starts, column)
        raw = dot(unsort_ref[here, :], small_all[...], ((1,), (1,)))
        raw = raw + head_row(dt_bias_ref)[0:1, :]
        lane = iota((1, LANES), 1)
        step = jnp.maximum(raw, 0.0) + jnp.log1p(jnp.exp(-jnp.abs(raw)))
        step = jnp.where(lane < heads, step, 0.0)
        rate = jnp.exp(head_row(a_log_ref)[0:1, :])
        decay = -rate * step
        lower = iota((BLOCK, BLOCK), 0) >= iota((BLOCK, BLOCK), 1)
        sums = jnp.dot(lower.astype(F32), decay, precision=HIGHEST, preferred_element_type=F32)
        sums_ref[here, :] = sums
        sums_t_ref[chunk] = sums.T[0:heads, :]
        step_t_ref[chunk] = step.T[0:heads, :]
        document_row = doc_at(starts, iota((1, BLOCK), 1) + origin)
        linked = lower & (document == document_row)
        scores_ref[chunk] = jnp.where(
            linked, dot(query_ref[here, LANES:], key_ref[here, :], ((1,), (1,))), 0.0
        )
        before_doc = jnp.where(origin > 0, doc_at(starts, origin - 1), 0)
        base_doc = jnp.where(base > 0, doc_at(starts, base - 1), 0)
        last_doc = doc_at(starts, origin + BLOCK - 1)
        carried_ref[here, :] = jnp.where(document == before_doc, jnp.exp(sums), 0.0)
        last = sums[BLOCK - 1 : BLOCK, :]
        closing = jnp.where(document == last_doc, jnp.exp(jnp.minimum(last - sums, 0.0)), 0.0) * step
        closing_ref[here, :] = closing
        before = before_ref[0:1, :]
        carry_ref[here, :] = jnp.where(document == base_doc, jnp.exp(before + sums), 0.0)
        before_ref[...] = jnp.broadcast_to(before + last, before_ref.shape)

    def scan(group, chunk):
        cols = slice(group * span, (group + 1) * span)
        here = block_of(chunk)
        keys, query = key_ref[here, :], query_ref[here, LANES:]
        inside = inside_ref[:, cols]
        carried_all = expanded(carried_ref[here, :], inside)
        state = state_ref[:, cols]
        x32 = x_ref[here, cols].astype(F32)
        y_ref[here, cols] = carried_all * dot_right(query, state) + skip_ref[0:1, cols] * x32
        weighted = expanded(closing_ref[here, :], inside) * x32
        state_ref[:, cols] = carried_all[BLOCK - 1 : BLOCK, :] * state + dot_turned(keys, weighted)
        scores = scores_ref[chunk]
        for head in range(group * group_heads, (group + 1) * group_heads):
            first, end = head * head_dim, (head + 1) * head_dim
            low, high = first // LANES * LANES, -(-end // LANES) * LANES
            gap = sums_ref[here, head : head + 1] - sums_t_ref[chunk, head : head + 1, :]
            weight = jnp.exp(jnp.minimum(gap, 0.0)) * step_t_ref[chunk, head : head + 1, :] * scores
            channel = iota((1, high - low), 1) + low
            x_own = x_ref[here, low:high].astype(F32)
            x_own = jnp.where((channel >= first) & (channel < end), x_own, 0.0).astype(BF16)
            y_ref[here, low:high] += dot_left(weight, x_own)

    def chain(group):
        cols = slice(group * span, (group + 1) * span)

        @pl.when(me > 0)
        def _():
            state_copy(group).wait_recv()

        @pl.when(me < shards - 1)
        def _():
            keep = expanded(carry_ref[rows - 8 : rows, :], inside_ref[:, cols])[7:8, :]
            passed = state_ref[:, cols]
            incoming = jnp.where(me > 0, state_in[group].astype(F32), 0.0)
            state_out[group] = (keep * incoming + passed).astype(BF16)
            state_copy(group).start()

        @pl.when(me > 0)
        def _():
            def add(chunk):
                here = block_of(chunk)
                carried = expanded(carry_ref[here, :], inside_ref[:, cols])
                y_ref[here, cols] += carried * dot(query_ref[here, LANES:], state_in[group])

            each(0, chunks, add)

    def gate_piece(j):
        col = pl.ds(pl.multiple_of(j * LANES, LANES), LANES)

        def rows_of(b):
            here = block_of(b)
            gate = dot(unsort_ref[here, :], came[pieces + j])
            gated = y_ref[here, col] * (gate * jax.nn.sigmoid(gate))
            y_ref[here, col] = gated
            square_ref[here, :] += gated * gated

        each(0, chunks, rows_of)
        store(j).start()

    pump(0)
    each(1, shards, lambda i: rim_copy(i).wait())
    rim_total = rim_in[0].astype(F32)
    for s in range(1, shards):
        rim_total = rim_total + rim_in[s].astype(F32)
    rim_ref[...] = rim_total

    def early(q):
        @pl.when(q > 0)
        def _():
            pump(q)

        x_piece(q)

        @pl.when(q < 2)
        def _():
            pick(pairs + q)

        @pl.when(q == 1)
        def _():
            each(1, peers, lambda i: wide_copy(i).wait())
            project()

        @pl.when((q == 2) | (q == 3))
        def _():
            each((q - 2) * (chunks // 2), (q - 1) * (chunks // 2), common)

    each(0, group_pieces, early)

    turn = 2 * jnp.minimum(me, chunks - 1)
    first_turn = group_pieces + chunks - 1
    last_turn = pieces + 1
    open_turn = last_turn + 3

    def finished(q):
        count = 2 * (q - open_turn + 1) - jnp.where(q >= open_turn + 2, 1, 0)
        return jnp.clip(count, 0, pieces)

    def late(q):
        @pl.when(q <= first_turn)
        def _():
            scan(0, q - group_pieces)

        @pl.when(q == first_turn + turn)
        def _():
            chain(0)

        @pl.when(q == last_turn + turn)
        def _():
            chain(1)

        pump(q)

        @pl.when(q < pieces)
        def _():
            x_piece(q)

        @pl.when(q < group_pieces + pairs - 2)
        def _():
            pick(pairs + 2 + q - group_pieces)

        @pl.when((q == pieces - 1) | (q == pieces))
        def _():
            half_chunks = chunks // 2
            each((q - pieces + 1) * half_chunks, (q - pieces + 2) * half_chunks, lambda c: scan(1, c))

        each(finished(q - 1), finished(q), gate_piece)

    each(group_pieces, 2 * pieces, late)

    high, low = halves(square_ref[...])
    ones = jnp.ones((16, LANES), BF16)
    total = dot(ones, high, ((1,), (1,))) + dot(ones, low, ((1,), (1,)))
    squares[own] = total[0:8, :]
    each(1, peers, lambda i: square_copy(i).start())

    def sent(q):
        each(1, shards, lambda i: piece_copy(q, i).wait_send())

    each(0, 2 * pieces, sent)

    @pl.when(me < shards - 1)
    def _():
        for group in range(GROUPS):
            state_copy(group).wait_send()

    each(0, pieces, lambda j: store(j).wait())
    each(1, peers, lambda i: square_copy(i).wait())
    total = squares[0]
    for peer in range(1, peers):
        total = total + squares[peer]
    total_ref[...] = total


def layer(lengths, a_log, dt_bias, d_skip, place, dt, conv_x, conv_bc, xs, gate, bc):
    shards, peers = lax.axis_size("seq"), lax.axis_size("head")
    rows, inner = xs.shape
    heads = a_log.shape[0]
    per = rows // shards
    half = per // (peers // 2)
    chunks = rows // BLOCK
    pieces = inner // LANES
    wide = 2 * LANES
    span = inner // GROUPS
    vmem = pl.BlockSpec(memory_space=pltpu.VMEM)
    hbm = pl.BlockSpec(memory_space=pl.ANY)
    return pl.pallas_call(
        functools.partial(layer_kernel, heads),
        in_specs=[pl.BlockSpec(memory_space=pltpu.SMEM)] * 4 + [vmem] * 4 + [hbm] * 3,
        out_specs=[hbm, vmem],
        out_shape=[jax.ShapeDtypeStruct((rows, inner), F32), jax.ShapeDtypeStruct((8, rows), F32)],
        scratch_shapes=[
            pltpu.VMEM((pieces, rows, wide), BF16),
            pltpu.VMEM((rows, wide), BF16),
            pltpu.VMEM((rows, rows), BF16),
            pltpu.VMEM((rows, rows), BF16),
            pltpu.VMEM((2 * pieces, rows, LANES), BF16),
            pltpu.VMEM((2 * pieces, rows, LANES), BF16),
            pltpu.VMEM((shards, heads + 16, per), BF16),
            pltpu.VMEM((shards, heads + 16, per), BF16),
            pltpu.VMEM((LANES, rows), BF16),
            pltpu.VMEM((shards * half, LANES), BF16),
            pltpu.VMEM((peers, shards * half, LANES), BF16),
            pltpu.VMEM((shards, TAIL, LANES), F32),
            pltpu.VMEM((shards, TAIL, LANES), BF16),
            pltpu.VMEM((shards, TAIL, LANES), BF16),
            pltpu.VMEM((TAIL, LANES), F32),
            pltpu.VMEM((RIM + rows, LANES), F32),
            pltpu.VMEM((rows, LANES), jnp.int32),
            pltpu.VMEM((LANES, inner), BF16),
            pltpu.VMEM((rows, inner), BF16),
            pltpu.VMEM((rows, LANES), BF16),
            pltpu.VMEM((rows, wide), BF16),
            pltpu.VMEM((rows, inner), F32),
            pltpu.VMEM((rows, LANES), F32),
            pltpu.VMEM((chunks, heads, BLOCK), F32),
            pltpu.VMEM((chunks, heads, BLOCK), F32),
            pltpu.VMEM((chunks, BLOCK, BLOCK), F32),
            pltpu.VMEM((rows, LANES), F32),
            pltpu.VMEM((rows, LANES), F32),
            pltpu.VMEM((rows, LANES), F32),
            pltpu.VMEM((8, LANES), F32),
            pltpu.VMEM((LANES, inner), F32),
            pltpu.VMEM((GROUPS, LANES, span), BF16),
            pltpu.VMEM((GROUPS, LANES, span), BF16),
            pltpu.VMEM((8, inner), F32),
            pltpu.VMEM((rows, LANES), F32),
            pltpu.VMEM((peers, 8, rows), F32),
            pltpu.SemaphoreType.DMA((pieces + 1,)),
            pltpu.SemaphoreType.DMA((2, 2 * pieces, shards)),
            pltpu.SemaphoreType.DMA((2, shards)),
            pltpu.SemaphoreType.DMA((2, shards)),
            pltpu.SemaphoreType.DMA((2, shards)),
            pltpu.SemaphoreType.DMA((2, peers)),
            pltpu.SemaphoreType.DMA((2, GROUPS)),
            pltpu.SemaphoreType.DMA((2, peers)),
            pltpu.SemaphoreType.DMA((pieces,)),
        ],
        compiler_params=pltpu.CompilerParams(
            collective_id=0, has_side_effects=True, vmem_limit_bytes=60 << 20
        ),
    )(lengths, a_log, dt_bias, d_skip, place, dt, conv_x, conv_bc, xs, gate, bc)


def scale_kernel(full_inner, total_ref, gain_ref, y_hbm, out_hbm, y_ref, out_ref, load_sems, store_sems):
    blocks = y_ref.shape[0] // LANES

    def load(k):
        here = block_of(k, LANES)
        return pltpu.make_async_copy(y_hbm.at[here], y_ref.at[here], load_sems.at[k])

    def store(k):
        here = block_of(k, LANES)
        return pltpu.make_async_copy(out_ref.at[here], out_hbm.at[here], store_sems.at[k])

    for k in range(blocks):
        load(k).start()
    gain = gain_ref[...].reshape(1, gain_ref.shape[0])
    scale = lax.rsqrt(total_ref[...] / full_inner + 1e-05)
    for k in range(blocks):
        here = block_of(k, LANES)
        column = jnp.concatenate([scale[:, here.start : here.start + LANES]] * (LANES // 8), 0).T[:, 0:1]
        load(k).wait()
        out_ref[here, :] = (y_ref[here, :] * column * gain).astype(BF16)
        store(k).start()
    for k in range(blocks):
        store(k).wait()


def scaled(y, total, gain, full_inner):
    rows, inner = y.shape
    vmem = pl.BlockSpec(memory_space=pltpu.VMEM)
    hbm = pl.BlockSpec(memory_space=pl.ANY)
    return pl.pallas_call(
        functools.partial(scale_kernel, full_inner),
        in_specs=[vmem, vmem, hbm],
        out_specs=hbm,
        out_shape=jax.ShapeDtypeStruct((rows, inner), BF16),
        scratch_shapes=[
            pltpu.VMEM((rows, inner), F32),
            pltpu.VMEM((rows, inner), BF16),
            pltpu.SemaphoreType.DMA((rows // LANES,)),
            pltpu.SemaphoreType.DMA((rows // LANES,)),
        ],
        compiler_params=pltpu.CompilerParams(vmem_limit_bytes=60 << 20),
    )(total, gain, y)


def body(
    xs, gate_in, bc_in, dt_in, placement, lengths,
    conv_x, conv_bc, a_log, dt_bias, d_skip, norm_gain, *, full_inner,
):
    y, total = layer(
        lengths, a_log, dt_bias, d_skip, placement[None, :], dt_in.T, conv_x, conv_bc, xs, gate_in, bc_in
    )
    return scaled(y, total, norm_gain, full_inner)


def solution(mesh):
    in_specs = (
        P(("parts", "seq"), "head"),
        P(("parts", "seq"), "head"),
        P(("parts", "seq"), None),
        P(("parts", "seq"), "head"),
        P(("parts", "seq")),
        P("parts"),
        P(None, "head"),
        P(),
        P("head"),
        P("head"),
        P("head"),
        P("head"),
    )
    out_specs = P(("parts", "seq"), "head")

    def whole(*args):
        step = functools.partial(body, full_inner=args[0].shape[1])
        return jax.shard_map(
            step, mesh=mesh, in_specs=in_specs, out_specs=out_specs, check_vma=False
        )(*args)

    return whole
```

```python
import functools

import jax
import jax.numpy as jnp
from jax import lax
from jax.experimental import pallas as pl
from jax.experimental.pallas import tpu as pltpu
from jax.sharding import PartitionSpec as P

BLOCK = 256
LANES = 128
RIM = 8
KERNEL_BYTES = 56800 << 10
GROUPS = 2
WINDOW = 2
BAND = 16
TAIL = 48
HIGHEST = lax.Precision.HIGHEST
MESH = pl.DeviceIdType.MESH
F32 = jnp.float32
BF16 = jnp.bfloat16


def iota(shape, dim):
    return lax.broadcasted_iota(jnp.int32, shape, dim)


def dot(a, b, dims=((1,), (0,))):
    return lax.dot_general(a, b, (dims, ((), ())), preferred_element_type=F32)


def halves(value):
    high = value.astype(BF16)
    return high, (value - high.astype(F32)).astype(BF16)


def dot_left(a, b):
    high, low = halves(a)
    return dot(high, b) + dot(low, b)


def dot_right(a, b):
    high, low = halves(b)
    return dot(jnp.concatenate([a, a], 1), jnp.concatenate([high, low], 0))


def dot_turned(a, b):
    high, low = halves(b)
    dims = ((0,), (0,))
    return dot(a, high, dims) + dot(a, low, dims)


def remote(source, target, sends, receives, axis, offset):
    count, me = lax.axis_size(axis), lax.axis_index(axis)
    return pltpu.make_async_remote_copy(
        src_ref=source,
        dst_ref=target,
        send_sem=sends,
        recv_sem=receives,
        device_id={axis: lax.rem(me + offset, count)},
        device_id_type=MESH,
    )


def each(first, last, action):
    def once(i, _):
        action(i)
        return 0

    lax.fori_loop(first, last, once, 0)


def doc_at(starts, position):
    total = jnp.where(starts[0] <= position, 1, 0)
    for start in starts[1:]:
        total = total + jnp.where(start <= position, 1, 0)
    return total


def starts_of(length_ref):
    starts = [jnp.int32(0)]
    for j in range(length_ref.shape[0] - 1):
        starts.append(starts[-1] + length_ref[j])
    return starts


def head_row(ref):
    lane = iota((8, LANES), 1)
    row = jnp.zeros((8, LANES), F32)
    for head in range(ref.shape[0]):
        row = jnp.where(lane == head, ref[head], row)
    return row


def expanded(value, inside):
    high, low = halves(value)
    low = pltpu.roll(low.astype(F32), LANES // 2, 1)
    lane = iota((1, LANES), 1)
    both = jnp.where(lane < LANES // 2, high.astype(F32), low)
    return dot(both.astype(BF16), inside)


def block_of(chunk, size=BLOCK):
    if isinstance(chunk, int):
        return pl.ds(chunk * size, size)
    return pl.ds(pl.multiple_of(chunk * size, size), size)


def one_hot(keys, first, count):
    return (iota((count, keys.shape[1]), 0) + first == keys).astype(F32).astype(BF16)


def slots_of(target, groups):
    rows = target.shape[1]
    chosen = (iota((groups, rows), 0) == target).astype(F32)
    before = (iota((LANES, LANES), 0) < iota((LANES, LANES), 1)).astype(F32).astype(BF16)
    blocks = [chosen[:, k : k + LANES] for k in range(0, rows, LANES)]
    inside = dot(jnp.concatenate(blocks, 0).astype(BF16), before)
    offset = jnp.zeros((groups, 1), F32)
    slots = []
    for k, block in enumerate(blocks):
        ranks = inside[k * groups : (k + 1) * groups, :] + offset
        slots.append(jnp.sum(block * ranks, axis=0, keepdims=True))
        offset = offset + jnp.sum(block, axis=1, keepdims=True)
    return jnp.concatenate(slots, 1).astype(jnp.int32)


def layer_kernel(
    heads, length_ref, a_log_ref, dt_bias_ref, d_skip_ref, place_ref, dt_ref, conv_x_ref, conv_bc_ref,
    x_hbm, gate_hbm, bc_hbm,
    y_ref, total_ref,
    given, bc_ref, sort_ref, unsort_ref, send, came, small_send, small_in, small_all,
    bc_send, bc_all, rim_rows, rim_send, rim_in, rim_ref, packed_ref, avail_ref, inside_ref,
    x_ref, key_ref, query_ref, sums_ref, sums_t_ref, step_t_ref, scores_ref,
    carried_ref, closing_ref, carry_ref, before_ref, state_ref, state_in, state_out, skip_ref,
    square_ref, squares,
    load_sems, sems, small_sems, bc_sems, rim_sems, wide_sems, state_sems, square_sems,
):
    shards, peers = lax.axis_size("seq"), lax.axis_size("head")
    me, own = lax.axis_index("seq"), lax.axis_index("head")
    rows, inner = y_ref.shape
    per = rows // shards
    half = per // (peers // 2)
    head_dim = inner // heads
    chunks = rows // BLOCK
    pieces = inner // LANES
    wide = 2 * LANES
    pairs = pieces // 2
    width = conv_x_ref.shape[0]
    group_heads = heads // GROUPS
    span = inner // GROUPS
    group_pieces = pieces // GROUPS
    base = me * rows
    mine = pl.ds(pl.multiple_of(me * per, per), per)
    starts = starts_of(length_ref)

    def load(pair):
        source = x_hbm if pair < pairs else gate_hbm
        first = (pair if pair < pairs else pair - pairs) * wide
        return pltpu.make_async_copy(source.at[:, first : first + wide], given.at[pair], load_sems.at[pair])

    bc_load = pltpu.make_async_copy(bc_hbm, bc_ref, load_sems.at[2 * pairs])

    def part(owner):
        return pl.ds(pl.multiple_of(owner * per, per), per)

    def piece_copy(q, i):
        return remote(
            send.at[q, part(lax.rem(me + i, shards))], came.at[q, mine],
            sems.at[0, q, i], sems.at[1, q, i], "seq", i,
        )

    def small_copy(i):
        return remote(
            small_send.at[lax.rem(me + i, shards)], small_in.at[me],
            small_sems.at[0, i], small_sems.at[1, i], "seq", i,
        )

    def bc_copy(i):
        dest = lax.rem(me + i, shards)
        return remote(
            bc_send.at[pl.ds(pl.multiple_of(dest * half, half), half)],
            bc_all.at[own, pl.ds(pl.multiple_of(me * half, half), half)],
            bc_sems.at[0, i], bc_sems.at[1, i], "seq", i,
        )

    def rim_copy(i):
        return remote(
            rim_send.at[lax.rem(me + i, shards)], rim_in.at[me],
            rim_sems.at[0, i], rim_sems.at[1, i], "seq", i,
        )

    def wide_copy(i):
        return remote(bc_all.at[own], bc_all.at[own], wide_sems.at[0, i], wide_sems.at[1, i], "head", i)

    def state_copy(group):
        return remote(
            state_out.at[group], state_in.at[group],
            state_sems.at[0, group], state_sems.at[1, group], "seq", 1,
        )

    def square_copy(i):
        return remote(
            squares.at[own], squares.at[own], square_sems.at[0, i], square_sems.at[1, i], "head", i
        )

    def start(q):
        each(1, shards, lambda i: piece_copy(q, i).start())

    def receive(q):
        each(1, shards, lambda i: piece_copy(q, i).wait_recv())

    for pair in range(2 * pairs):
        load(pair).start()
        if pair == 0:
            bc_load.start()
    barrier = pltpu.get_barrier_semaphore()
    for axis in ("seq", "head"):
        count, here = lax.axis_size(axis), lax.axis_index(axis)

        def signal(i, axis=axis, count=count, here=here):
            pl.semaphore_signal(
                barrier, inc=1, device_id={axis: lax.rem(here + i, count)}, device_id_type=MESH
            )

        each(1, count, signal)

    place = place_ref[0:1, :]
    target = lax.shift_right_logical(place, rows.bit_length() - 1)
    local = place & (rows - 1)
    slot = slots_of(target, -(-shards // 16) * 16)
    key = target * per + slot

    def sort_rows(b):
        sort_ref[block_of(b), :] = one_hot(key, b * BLOCK, BLOCK)

    each(0, chunks, sort_rows)

    def pick(pair):
        def rows_of(b):
            value = dot(sort_ref[block_of(b), :], given[pair]).astype(BF16)
            send[2 * pair, block_of(b), :] = value[:, :LANES]
            send[2 * pair + 1, block_of(b), :] = value[:, LANES:]

        each(0, chunks, rows_of)
        for q in (2 * pair, 2 * pair + 1):
            came[q, mine, :] = send[q, mine, :]

    load(0).wait()
    pick(0)
    pl.semaphore_wait(barrier, shards - 1 + peers - 1)
    start(0)

    digits = jnp.concatenate(
        [
            dt_ref[...],
            jnp.where(
                iota((16, rows), 0) == 0, local >> 5, jnp.where(iota((16, rows), 0) == 1, local & 31, 0)
            ).astype(F32).astype(BF16),
        ],
        0,
    )

    def small_rows(d):
        small_send[d] = dot(digits, sort_ref[part(d), :], ((1,), (1,))).astype(BF16)

    each(0, shards, small_rows)
    small_in[me] = small_send[me]
    bc_load.wait()
    bc_cols = pl.ds(pl.multiple_of(lax.rem(own, 2) * LANES, LANES), LANES)
    bc_first = own // 2 * half

    def bc_rows(d):
        source = sort_ref[pl.ds(pl.multiple_of(d * per + bc_first, half), half), :]
        bc_send[pl.ds(pl.multiple_of(d * half, half), half), :] = dot(source, bc_ref[:, bc_cols]).astype(BF16)

    each(0, shards, bc_rows)
    bc_mine = pl.ds(pl.multiple_of(me * half, half), half)
    bc_all[own, bc_mine, :] = bc_send[bc_mine, :]

    each(1, shards, lambda i: small_copy(i).start())
    each(1, shards, lambda i: bc_copy(i).start())
    start(1)

    line = iota((RIM * shards, 1), 0)
    back = line & (RIM - 1)
    wanted = lax.shift_right_logical(line, RIM.bit_length() - 1) * rows - (width - 1) + back
    wanted = jnp.where((back < width - 1) & (wanted >= 0), wanted, -1)
    rim_pick = (wanted == place).astype(F32).astype(BF16)
    rim_rows[...] = jnp.zeros_like(rim_rows)

    def rim_put(value, j):
        for d in range(shards):
            for k in range(width - 1):
                rim_rows[d, pl.ds(k * BAND + j, 1), :] = value[d * RIM + k : d * RIM + k + 1, :]

    def rim_of(value, j):
        rim_put(value[:, :LANES], j)
        rim_put(value[:, LANES:], j + 1)

    rim_of(dot(rim_pick, bc_ref[...]), pieces)
    for pair in range(1, pairs):
        load(pair).wait()
    each(0, pairs, lambda pair: rim_of(dot(rim_pick, given[pair]), 2 * pair))
    rim_send[...] = rim_rows[...].astype(BF16)
    rim_in[me] = rim_send[me]
    each(1, shards, lambda i: rim_copy(i).start())
    each(1, pairs, pick)

    for b in range(chunks):
        position = iota((BLOCK, 1), 0) + (base + b * BLOCK)
        first = jnp.zeros((BLOCK, 1), jnp.int32)
        for begin in starts[1:]:
            first = jnp.where(begin <= position, begin, first)
        avail_ref[b * BLOCK : (b + 1) * BLOCK, :] = jnp.broadcast_to(position - first, (BLOCK, LANES))
    head, channel = iota((LANES, inner), 0), iota((LANES, inner), 1)
    head = jnp.where(head < LANES // 2, head, head - LANES // 2)
    inside = (channel >= head * head_dim) & (channel < (head + 1) * head_dim)
    inside_ref[...] = inside.astype(F32).astype(BF16)
    skip_ref[...] = expanded(head_row(d_skip_ref), inside_ref[...])
    state_ref[...] = jnp.zeros_like(state_ref)
    before_ref[...] = jnp.zeros_like(before_ref)
    square_ref[...] = jnp.zeros_like(square_ref)
    small_all[...] = jnp.zeros_like(small_all)

    def pump(q):
        receive(q)
        if isinstance(q, int):
            if q + WINDOW < 2 * pieces:
                start(q + WINDOW)
        else:

            @pl.when(q + WINDOW < 2 * pieces)
            def _():
                start(q + WINDOW)

    pump(0)
    each(1, shards, lambda i: bc_copy(i).wait())
    each(1, peers, lambda i: wide_copy(i).start())
    each(1, shards, lambda i: small_copy(i).wait())
    lines = small_in.shape[1]
    if per % LANES == 0:
        for s in range(shards):
            small_all[0:lines, s * per : (s + 1) * per] = small_in[s]
    else:
        total = jnp.zeros((lines, rows), F32)
        for s in range(shards):
            spread = (iota((per, rows), 0) + s * per == iota((per, rows), 1)).astype(F32).astype(BF16)
            total = total + dot(small_in[s], spread)
        small_all[0:lines, :] = total.astype(BF16)
    high = small_all[heads : heads + 1, :].astype(F32)
    low = small_all[heads + 1 : heads + 2, :].astype(F32)
    landed = (high * 32.0 + low).astype(jnp.int32)

    def unsort_rows(b):
        unsort_ref[block_of(b), :] = one_hot(landed, b * BLOCK, BLOCK)

    each(0, chunks, unsort_rows)

    def convolve(value, j, taps_ref, col, out_ref):
        packed_ref[RIM:, :] = value
        for k in range(width - 1):
            packed_ref[RIM - (width - 1) + k : RIM - (width - 1) + k + 1, :] = rim_ref[pl.ds(k * BAND + j, 1), :]
        taps = taps_ref[:, col]
        total = taps[0:1, :] * packed_ref[RIM:, :]
        for lag in range(1, width):
            moved = taps[lag : lag + 1, :] * packed_ref[RIM - lag : RIM - lag + rows, :]
            total = total + jnp.where(avail_ref[...] >= lag, moved, 0.0)
        out_ref[:, col] = (total * jax.nn.sigmoid(total)).astype(BF16)

    def x_piece(j):
        col = pl.ds(pl.multiple_of(j * LANES, LANES), LANES)
        convolve(dot(unsort_ref[...], came[j]), j, conv_x_ref, col, x_ref)

    for pair in range(pairs, 2 * pairs):
        load(pair).wait()
    def project():
        for side in range(2):
            quarters = [bc_all[2 * r + side].reshape(shards, half, LANES) for r in range(peers // 2)]
            together = jnp.concatenate(quarters, 1).reshape(rows, LANES)
            value = dot(unsort_ref[...], together)
            here = slice(side * LANES, (side + 1) * LANES)
            if side == 0:
                convolve(value, pieces, conv_bc_ref, here, key_ref)
            else:
                convolve(value, pieces + 1, conv_bc_ref, here, query_ref)

    def common(chunk):
        origin = base + chunk * BLOCK
        here = block_of(chunk)
        column = iota((BLOCK, 1), 0) + origin
        document = doc_at(starts, column)
        raw = dot(unsort_ref[here, :], small_all[...], ((1,), (1,)))
        raw = raw + head_row(dt_bias_ref)[0:1, :]
        lane = iota((1, LANES), 1)
        step = jnp.maximum(raw, 0.0) + jnp.log1p(jnp.exp(-jnp.abs(raw)))
        step = jnp.where(lane < heads, step, 0.0)
        rate = jnp.exp(head_row(a_log_ref)[0:1, :])
        decay = -rate * step
        lower = iota((BLOCK, BLOCK), 0) >= iota((BLOCK, BLOCK), 1)
        sums = jnp.dot(lower.astype(F32), decay, precision=HIGHEST, preferred_element_type=F32)
        sums_ref[here, :] = sums
        sums_t_ref[chunk] = sums.T[0:heads, :]
        step_t_ref[chunk] = step.T[0:heads, :]
        document_row = doc_at(starts, iota((1, BLOCK), 1) + origin)
        linked = lower & (document == document_row)
        scores_ref[chunk] = jnp.where(
            linked, dot(query_ref[here, LANES:], key_ref[here, :], ((1,), (1,))), 0.0
        )
        before_doc = jnp.where(origin > 0, doc_at(starts, origin - 1), 0)
        base_doc = jnp.where(base > 0, doc_at(starts, base - 1), 0)
        last_doc = doc_at(starts, origin + BLOCK - 1)
        carried_ref[here, :] = jnp.where(document == before_doc, jnp.exp(sums), 0.0)
        last = sums[BLOCK - 1 : BLOCK, :]
        closing = jnp.where(document == last_doc, jnp.exp(jnp.minimum(last - sums, 0.0)), 0.0) * step
        closing_ref[here, :] = closing
        before = before_ref[0:1, :]
        carry_ref[here, :] = jnp.where(document == base_doc, jnp.exp(before + sums), 0.0)
        before_ref[...] = jnp.broadcast_to(before + last, before_ref.shape)

    def scan(group, chunk):
        cols = slice(group * span, (group + 1) * span)
        here = block_of(chunk)
        keys, query = key_ref[here, :], query_ref[here, LANES:]
        inside = inside_ref[:, cols]
        carried_all = expanded(carried_ref[here, :], inside)
        state = state_ref[:, cols]
        x32 = x_ref[here, cols].astype(F32)
        y_ref[here, cols] = carried_all * dot_right(query, state) + skip_ref[0:1, cols] * x32
        weighted = expanded(closing_ref[here, :], inside) * x32
        state_ref[:, cols] = carried_all[BLOCK - 1 : BLOCK, :] * state + dot_turned(keys, weighted)
        scores = scores_ref[chunk]
        for head in range(group * group_heads, (group + 1) * group_heads):
            first, end = head * head_dim, (head + 1) * head_dim
            low, high = first // LANES * LANES, -(-end // LANES) * LANES
            gap = sums_ref[here, head : head + 1] - sums_t_ref[chunk, head : head + 1, :]
            weight = jnp.exp(jnp.minimum(gap, 0.0)) * step_t_ref[chunk, head : head + 1, :] * scores
            channel = iota((1, high - low), 1) + low
            x_own = x_ref[here, low:high].astype(F32)
            x_own = jnp.where((channel >= first) & (channel < end), x_own, 0.0).astype(BF16)
            y_ref[here, low:high] += dot_left(weight, x_own)

    def chain(group):
        cols = slice(group * span, (group + 1) * span)

        @pl.when(me > 0)
        def _():
            state_copy(group).wait_recv()

        @pl.when(me < shards - 1)
        def _():
            keep = expanded(carry_ref[rows - 8 : rows, :], inside_ref[:, cols])[7:8, :]
            passed = state_ref[:, cols]
            incoming = jnp.where(me > 0, state_in[group].astype(F32), 0.0)
            state_out[group] = (keep * incoming + passed).astype(BF16)
            state_copy(group).start()

        @pl.when(me > 0)
        def _():
            def add(chunk):
                here = block_of(chunk)
                carried = expanded(carry_ref[here, :], inside_ref[:, cols])
                y_ref[here, cols] += carried * dot(query_ref[here, LANES:], state_in[group])

            each(0, chunks, add)

    def gate_piece(j):
        col = pl.ds(pl.multiple_of(j * LANES, LANES), LANES)

        def rows_of(b):
            here = block_of(b)
            gate = dot(unsort_ref[here, :], came[pieces + j])
            gated = y_ref[here, col] * (gate * jax.nn.sigmoid(gate))
            y_ref[here, col] = gated
            square_ref[here, :] += gated * gated

        each(0, chunks, rows_of)

    each(1, shards, lambda i: rim_copy(i).wait())
    rim_total = rim_in[0].astype(F32)
    for s in range(1, shards):
        rim_total = rim_total + rim_in[s].astype(F32)
    rim_ref[...] = rim_total

    def early(q):
        @pl.when(q > 0)
        def _():
            pump(q)

        x_piece(q)

        @pl.when(q < 2)
        def _():
            pick(pairs + q)

        @pl.when(q == 1)
        def _():
            each(1, peers, lambda i: wide_copy(i).wait())
            project()

        @pl.when((q == 2) | (q == 3))
        def _():
            each((q - 2) * (chunks // 2), (q - 1) * (chunks // 2), common)

    each(0, group_pieces, early)

    turn = 2 * jnp.minimum(me, chunks - 1)
    first_turn = group_pieces + chunks - 1
    last_turn = pieces + 1
    open_turn = last_turn + 3

    def finished(q):
        count = 2 * (q - open_turn + 1) - jnp.where(q >= open_turn + 2, 1, 0)
        return jnp.clip(count, 0, pieces)

    def late(q):
        @pl.when(q <= first_turn)
        def _():
            scan(0, q - group_pieces)

        @pl.when(q == first_turn + turn)
        def _():
            chain(0)

        @pl.when(q == last_turn + turn)
        def _():
            chain(1)

        pump(q)

        @pl.when(q < pieces)
        def _():
            x_piece(q)

        @pl.when(q < group_pieces + pairs - 2)
        def _():
            pick(pairs + 2 + q - group_pieces)

        @pl.when((q == pieces - 1) | (q == pieces))
        def _():
            half_chunks = chunks // 2
            each((q - pieces + 1) * half_chunks, (q - pieces + 2) * half_chunks, lambda c: scan(1, c))

        each(finished(q - 1), finished(q), gate_piece)

    each(group_pieces, 2 * pieces, late)

    high, low = halves(square_ref[...])
    ones = jnp.ones((16, LANES), BF16)
    total = dot(ones, high, ((1,), (1,))) + dot(ones, low, ((1,), (1,)))
    squares[own] = total[0:8, :]
    each(1, peers, lambda i: square_copy(i).start())

    def sent(q):
        each(1, shards, lambda i: piece_copy(q, i).wait_send())

    each(0, 2 * pieces, sent)

    @pl.when(me < shards - 1)
    def _():
        for group in range(GROUPS):
            state_copy(group).wait_send()

    each(1, peers, lambda i: square_copy(i).wait())
    total = squares[0]
    for peer in range(1, peers):
        total = total + squares[peer]
    total_ref[...] = total


def layer(lengths, a_log, dt_bias, d_skip, place, dt, conv_x, conv_bc, xs, gate, bc):
    shards, peers = lax.axis_size("seq"), lax.axis_size("head")
    rows, inner = xs.shape
    heads = a_log.shape[0]
    per = rows // shards
    half = per // (peers // 2)
    chunks = rows // BLOCK
    pieces = inner // LANES
    wide = 2 * LANES
    span = inner // GROUPS
    vmem = pl.BlockSpec(memory_space=pltpu.VMEM)
    hbm = pl.BlockSpec(memory_space=pltpu.HBM)
    return pl.pallas_call(
        functools.partial(layer_kernel, heads),
        in_specs=[pl.BlockSpec(memory_space=pltpu.SMEM)] * 4 + [vmem] * 4 + [hbm] * 3,
        out_specs=[vmem, vmem],
        out_shape=[pltpu.VMEM((rows, inner), F32), pltpu.VMEM((8, rows), F32)],
        scratch_shapes=[
            pltpu.VMEM((pieces, rows, wide), BF16),
            pltpu.VMEM((rows, wide), BF16),
            pltpu.VMEM((rows, rows), BF16),
            pltpu.VMEM((rows, rows), BF16),
            pltpu.VMEM((2 * pieces, rows, LANES), BF16),
            pltpu.VMEM((2 * pieces, rows, LANES), BF16),
            pltpu.VMEM((shards, heads + 16, per), BF16),
            pltpu.VMEM((shards, heads + 16, per), BF16),
            pltpu.VMEM((LANES, rows), BF16),
            pltpu.VMEM((shards * half, LANES), BF16),
            pltpu.VMEM((peers, shards * half, LANES), BF16),
            pltpu.VMEM((shards, TAIL, LANES), F32),
            pltpu.VMEM((shards, TAIL, LANES), BF16),
            pltpu.VMEM((shards, TAIL, LANES), BF16),
            pltpu.VMEM((TAIL, LANES), F32),
            pltpu.VMEM((RIM + rows, LANES), F32),
            pltpu.VMEM((rows, LANES), jnp.int32),
            pltpu.VMEM((LANES, inner), BF16),
            pltpu.VMEM((rows, inner), BF16),
            pltpu.VMEM((rows, LANES), BF16),
            pltpu.VMEM((rows, wide), BF16),
            pltpu.VMEM((rows, LANES), F32),
            pltpu.VMEM((chunks, heads, BLOCK), F32),
            pltpu.VMEM((chunks, heads, BLOCK), F32),
            pltpu.VMEM((chunks, BLOCK, BLOCK), F32),
            pltpu.VMEM((rows, LANES), F32),
            pltpu.VMEM((rows, LANES), F32),
            pltpu.VMEM((rows, LANES), F32),
            pltpu.VMEM((8, LANES), F32),
            pltpu.VMEM((LANES, inner), F32),
            pltpu.VMEM((GROUPS, LANES, span), BF16),
            pltpu.VMEM((GROUPS, LANES, span), BF16),
            pltpu.VMEM((8, inner), F32),
            pltpu.VMEM((rows, LANES), F32),
            pltpu.VMEM((peers, 8, rows), F32),
            pltpu.SemaphoreType.DMA((pieces + 1,)),
            pltpu.SemaphoreType.DMA((2, 2 * pieces, shards)),
            pltpu.SemaphoreType.DMA((2, shards)),
            pltpu.SemaphoreType.DMA((2, shards)),
            pltpu.SemaphoreType.DMA((2, shards)),
            pltpu.SemaphoreType.DMA((2, peers)),
            pltpu.SemaphoreType.DMA((2, GROUPS)),
            pltpu.SemaphoreType.DMA((2, peers)),
        ],
        compiler_params=pltpu.CompilerParams(
            collective_id=0, has_side_effects=True, vmem_limit_bytes=KERNEL_BYTES
        ),
    )(lengths, a_log, dt_bias, d_skip, place, dt, conv_x, conv_bc, xs, gate, bc)


def scale_kernel(full_inner, y_ref, total_ref, gain_ref, out_hbm, out_ref, store_sems):
    blocks = y_ref.shape[0] // LANES

    def store(k):
        here = block_of(k, LANES)
        return pltpu.make_async_copy(out_ref.at[here], out_hbm.at[here], store_sems.at[k])

    gain = gain_ref[...].reshape(1, gain_ref.shape[0])
    scale = lax.rsqrt(total_ref[...] / full_inner + 1e-05)
    for k in range(blocks):
        here = block_of(k, LANES)
        column = jnp.concatenate([scale[:, here.start : here.start + LANES]] * (LANES // 8), 0).T[:, 0:1]
        out_ref[here, :] = (y_ref[here, :] * column * gain).astype(BF16)
        store(k).start()
    for k in range(blocks):
        store(k).wait()


def scaled(y, total, gain, full_inner):
    rows, inner = y.shape
    vmem = pl.BlockSpec(memory_space=pltpu.VMEM)
    return pl.pallas_call(
        functools.partial(scale_kernel, full_inner),
        in_specs=[vmem, vmem, vmem],
        out_specs=pl.BlockSpec(memory_space=pltpu.HBM),
        out_shape=jax.ShapeDtypeStruct((rows, inner), BF16),
        scratch_shapes=[
            pltpu.VMEM((rows, inner), BF16),
            pltpu.SemaphoreType.DMA((rows // LANES,)),
        ],
        compiler_params=pltpu.CompilerParams(vmem_limit_bytes=KERNEL_BYTES),
    )(
        pltpu.with_memory_space_constraint(y, pltpu.VMEM),
        pltpu.with_memory_space_constraint(total, pltpu.VMEM),
        gain,
    )


def body(
    xs, gate_in, bc_in, dt_in, placement, lengths,
    conv_x, conv_bc, a_log, dt_bias, d_skip, norm_gain, *, full_inner,
):
    y, total = layer(
        lengths, a_log, dt_bias, d_skip, placement[None, :], dt_in.T, conv_x, conv_bc, xs, gate_in, bc_in
    )
    return scaled(y, total, norm_gain, full_inner)


def solution(mesh):
    in_specs = (
        P(("parts", "seq"), "head"),
        P(("parts", "seq"), "head"),
        P(("parts", "seq"), None),
        P(("parts", "seq"), "head"),
        P(("parts", "seq")),
        P("parts"),
        P(None, "head"),
        P(),
        P("head"),
        P("head"),
        P("head"),
        P("head"),
    )
    out_specs = P(("parts", "seq"), "head")

    def whole(*args):
        step = functools.partial(body, full_inner=args[0].shape[1])
        return jax.shard_map(
            step, mesh=mesh, in_specs=in_specs, out_specs=out_specs, check_vma=False
        )(*args)

    return whole
```

```python
import functools

import jax
import jax.numpy as jnp
from jax import lax
from jax.experimental import pallas as pl
from jax.experimental.pallas import tpu as pltpu
from jax.sharding import PartitionSpec as P

BLOCK = 256
LANES = 128
RIM = 8
KERNEL_BYTES = 56800 << 10
GROUPS = 2
WINDOW = 2
BAND = 16
TAIL = 48
HIGHEST = lax.Precision.HIGHEST
MESH = pl.DeviceIdType.MESH
F32 = jnp.float32
BF16 = jnp.bfloat16


def iota(shape, dim):
    return lax.broadcasted_iota(jnp.int32, shape, dim)


def dot(a, b, dims=((1,), (0,))):
    return lax.dot_general(a, b, (dims, ((), ())), preferred_element_type=F32)


def halves(value):
    high = value.astype(BF16)
    return high, (value - high.astype(F32)).astype(BF16)


def dot_left(a, b):
    high, low = halves(a)
    return dot(high, b) + dot(low, b)


def dot_right(a, b):
    high, low = halves(b)
    return dot(jnp.concatenate([a, a], 1), jnp.concatenate([high, low], 0))


def dot_turned(a, b):
    high, low = halves(b)
    dims = ((0,), (0,))
    return dot(a, high, dims) + dot(a, low, dims)


def remote(source, target, sends, receives, axis, offset):
    count, me = lax.axis_size(axis), lax.axis_index(axis)
    return pltpu.make_async_remote_copy(
        src_ref=source,
        dst_ref=target,
        send_sem=sends,
        recv_sem=receives,
        device_id={axis: lax.rem(me + offset, count)},
        device_id_type=MESH,
    )


def each(first, last, action):
    def once(i, _):
        action(i)
        return 0

    lax.fori_loop(first, last, once, 0)


def doc_at(starts, position):
    total = jnp.where(starts[0] <= position, 1, 0)
    for start in starts[1:]:
        total = total + jnp.where(start <= position, 1, 0)
    return total


def starts_of(length_ref):
    starts = [jnp.int32(0)]
    for j in range(length_ref.shape[0] - 1):
        starts.append(starts[-1] + length_ref[j])
    return starts


def head_row(ref):
    lane = iota((8, LANES), 1)
    row = jnp.zeros((8, LANES), F32)
    for head in range(ref.shape[0]):
        row = jnp.where(lane == head, ref[head], row)
    return row


def expanded(value, inside):
    high, low = halves(value)
    low = pltpu.roll(low.astype(F32), LANES // 2, 1)
    lane = iota((1, LANES), 1)
    both = jnp.where(lane < LANES // 2, high.astype(F32), low)
    return dot(both.astype(BF16), inside)


def block_of(chunk, size=BLOCK):
    if isinstance(chunk, int):
        return pl.ds(chunk * size, size)
    return pl.ds(pl.multiple_of(chunk * size, size), size)


def one_hot(keys, first, count):
    return (iota((count, keys.shape[1]), 0) + first == keys).astype(F32).astype(BF16)


def slots_of(target, groups):
    rows = target.shape[1]
    chosen = (iota((groups, rows), 0) == target).astype(F32)
    before = (iota((LANES, LANES), 0) < iota((LANES, LANES), 1)).astype(F32).astype(BF16)
    blocks = [chosen[:, k : k + LANES] for k in range(0, rows, LANES)]
    inside = dot(jnp.concatenate(blocks, 0).astype(BF16), before)
    offset = jnp.zeros((groups, 1), F32)
    slots = []
    for k, block in enumerate(blocks):
        ranks = inside[k * groups : (k + 1) * groups, :] + offset
        slots.append(jnp.sum(block * ranks, axis=0, keepdims=True))
        offset = offset + jnp.sum(block, axis=1, keepdims=True)
    return jnp.concatenate(slots, 1).astype(jnp.int32)


def layer_kernel(
    heads, length_ref, a_log_ref, dt_bias_ref, d_skip_ref, place_ref, dt_ref, conv_x_ref, conv_bc_ref, gain_ref,
    x_hbm, gate_hbm, bc_hbm,
    y_ref, total_ref,
    given, bc_ref, sort_ref, unsort_ref, send, came, small_send, small_in, small_all,
    bc_send, bc_all, rim_rows, rim_send, rim_in, rim_ref, packed_ref, avail_ref, inside_ref,
    x_ref, key_ref, query_ref, sums_ref, sums_t_ref, step_t_ref, scores_ref,
    carried_ref, closing_ref, carry_ref, before_ref, state_ref, state_in, state_out, skip_ref, gain_line,
    square_ref, squares,
    load_sems, sems, small_sems, bc_sems, rim_sems, wide_sems, state_sems, square_sems,
):
    shards, peers = lax.axis_size("seq"), lax.axis_size("head")
    me, own = lax.axis_index("seq"), lax.axis_index("head")
    rows, inner = y_ref.shape
    per = rows // shards
    half = per // (peers // 2)
    head_dim = inner // heads
    chunks = rows // BLOCK
    pieces = inner // LANES
    wide = 2 * LANES
    pairs = pieces // 2
    width = conv_x_ref.shape[0]
    group_heads = heads // GROUPS
    span = inner // GROUPS
    group_pieces = pieces // GROUPS
    base = me * rows
    lanes = min(per, LANES)
    lines = per // lanes
    spare = pieces + 2
    mine = pl.ds(pl.multiple_of(me * per, per), per)
    starts = starts_of(length_ref)

    def load(pair):
        source = x_hbm if pair < pairs else gate_hbm
        first = (pair if pair < pairs else pair - pairs) * wide
        return pltpu.make_async_copy(source.at[:, first : first + wide], given.at[pair], load_sems.at[pair])

    bc_load = pltpu.make_async_copy(bc_hbm, bc_ref, load_sems.at[2 * pairs])

    def part(owner):
        return pl.ds(pl.multiple_of(owner * per, per), per)

    def piece_copy(q, i):
        return remote(
            send.at[q, part(lax.rem(me + i, shards))], came.at[q, mine],
            sems.at[0, q, i], sems.at[1, q, i], "seq", i,
        )

    def small_copy(i):
        return remote(
            small_send.at[lax.rem(me + i, shards)], small_in.at[me],
            small_sems.at[0, i], small_sems.at[1, i], "seq", i,
        )

    def bc_copy(i):
        dest = lax.rem(me + i, shards)
        return remote(
            bc_send.at[pl.ds(pl.multiple_of(dest * half, half), half)],
            bc_all.at[own, pl.ds(pl.multiple_of(me * half, half), half)],
            bc_sems.at[0, i], bc_sems.at[1, i], "seq", i,
        )

    def rim_copy(i):
        return remote(
            rim_send.at[lax.rem(me + i, shards)], rim_in.at[me],
            rim_sems.at[0, i], rim_sems.at[1, i], "seq", i,
        )

    def wide_copy(i):
        return remote(bc_all.at[own], bc_all.at[own], wide_sems.at[0, i], wide_sems.at[1, i], "head", i)

    def state_copy(group):
        return remote(
            state_out.at[group], state_in.at[group],
            state_sems.at[0, group], state_sems.at[1, group], "seq", 1,
        )

    def square_copy(i):
        return remote(
            squares.at[own], squares.at[own], square_sems.at[0, i], square_sems.at[1, i], "head", i
        )

    def start(q):
        each(1, shards, lambda i: piece_copy(q, i).start())

    def receive(q):
        each(1, shards, lambda i: piece_copy(q, i).wait_recv())

    for pair in range(2 * pairs):
        load(pair).start()
        if pair == 0:
            bc_load.start()
    barrier = pltpu.get_barrier_semaphore()
    for axis in ("seq", "head"):
        count, here = lax.axis_size(axis), lax.axis_index(axis)

        def signal(i, axis=axis, count=count, here=here):
            pl.semaphore_signal(
                barrier, inc=1, device_id={axis: lax.rem(here + i, count)}, device_id_type=MESH
            )

        each(1, count, signal)

    place = place_ref[0:1, :]
    target = lax.shift_right_logical(place, rows.bit_length() - 1)
    local = place & (rows - 1)
    slot = slots_of(target, -(-shards // 16) * 16)
    key = target * per + slot

    def sort_rows(b):
        sort_ref[block_of(b), :] = one_hot(key, b * BLOCK, BLOCK)

    each(0, chunks, sort_rows)

    def pick(pair):
        def rows_of(b):
            value = dot(sort_ref[block_of(b), :], given[pair]).astype(BF16)
            send[2 * pair, block_of(b), :] = value[:, :LANES]
            send[2 * pair + 1, block_of(b), :] = value[:, LANES:]

        each(0, chunks, rows_of)
        for q in (2 * pair, 2 * pair + 1):
            came[q, mine, :] = send[q, mine, :]

    load(0).wait()
    pick(0)
    pl.semaphore_wait(barrier, shards - 1 + peers - 1)
    start(0)

    rim_rows[...] = jnp.zeros_like(rim_rows)
    digits = jnp.where(iota((16, rows), 0) == 0, local >> 5, local & 31).astype(F32).astype(BF16)
    digits = jnp.concatenate([dt_ref[...], digits], 0)

    def small_rows(d):
        values = dot(digits, sort_ref[part(d), :], ((1,), (1,)))
        small_send[d] = values[0:heads, :].astype(BF16)
        for k in range(2):
            for line in range(lines):
                rim_rows[d, k * BAND + spare + line : k * BAND + spare + line + 1, 0:lanes] = values[
                    heads + k : heads + k + 1, line * lanes : (line + 1) * lanes
                ]

    each(0, shards, small_rows)
    small_in[me] = small_send[me]
    bc_load.wait()
    bc_cols = pl.ds(pl.multiple_of(lax.rem(own, 2) * LANES, LANES), LANES)
    bc_first = own // 2 * half

    def bc_rows(d):
        source = sort_ref[pl.ds(pl.multiple_of(d * per + bc_first, half), half), :]
        bc_send[pl.ds(pl.multiple_of(d * half, half), half), :] = dot(source, bc_ref[:, bc_cols]).astype(BF16)

    each(0, shards, bc_rows)
    bc_mine = pl.ds(pl.multiple_of(me * half, half), half)
    bc_all[own, bc_mine, :] = bc_send[bc_mine, :]

    each(1, shards, lambda i: small_copy(i).start())
    each(1, shards, lambda i: bc_copy(i).start())

    line = iota((RIM * shards, 1), 0)
    back = line & (RIM - 1)
    wanted = lax.shift_right_logical(line, RIM.bit_length() - 1) * rows - (width - 1) + back
    wanted = jnp.where((back < width - 1) & (wanted >= 0), wanted, -1)
    rim_pick = (wanted == place).astype(F32).astype(BF16)

    def rim_put(value, j):
        for d in range(shards):
            for k in range(width - 1):
                rim_rows[d, pl.ds(k * BAND + j, 1), :] = value[d * RIM + k : d * RIM + k + 1, :]

    def rim_of(value, j):
        rim_put(value[:, :LANES], j)
        rim_put(value[:, LANES:], j + 1)

    rim_of(dot(rim_pick, bc_ref[...]), pieces)
    for pair in range(1, pairs):
        load(pair).wait()
    each(0, pairs, lambda pair: rim_of(dot(rim_pick, given[pair]), 2 * pair))
    rim_send[...] = rim_rows[...].astype(BF16)
    rim_in[me] = rim_send[me]
    each(1, shards, lambda i: rim_copy(i).start())
    start(1)
    each(1, pairs, pick)

    for b in range(chunks):
        position = iota((BLOCK, 1), 0) + (base + b * BLOCK)
        first = jnp.zeros((BLOCK, 1), jnp.int32)
        for begin in starts[1:]:
            first = jnp.where(begin <= position, begin, first)
        avail_ref[b * BLOCK : (b + 1) * BLOCK, :] = jnp.broadcast_to(position - first, (BLOCK, LANES))
    head, channel = iota((LANES, inner), 0), iota((LANES, inner), 1)
    head = jnp.where(head < LANES // 2, head, head - LANES // 2)
    inside = (channel >= head * head_dim) & (channel < (head + 1) * head_dim)
    inside_ref[...] = inside.astype(F32).astype(BF16)
    gain_line[...] = jnp.broadcast_to(gain_ref[...].reshape(1, inner), gain_line.shape)
    skip_ref[...] = expanded(head_row(d_skip_ref), inside_ref[...])
    state_ref[...] = jnp.zeros_like(state_ref)
    before_ref[...] = jnp.zeros_like(before_ref)
    square_ref[...] = jnp.zeros_like(square_ref)
    small_all[...] = jnp.zeros_like(small_all)

    def ahead(q):
        return jnp.minimum(q + 1 + WINDOW + jnp.where(q >= 2 * pieces - 6, 2, 0), 2 * pieces)

    def pump(q):
        receive(q)
        each(jnp.where(q > 0, ahead(q - 1), WINDOW), ahead(q), start)

    pump(0)
    each(1, shards, lambda i: bc_copy(i).wait())
    each(1, peers, lambda i: wide_copy(i).start())
    each(1, shards, lambda i: small_copy(i).wait())
    each(1, shards, lambda i: rim_copy(i).wait())
    wide_lines = []
    for s in range(shards):
        rim = rim_in[s].astype(F32)
        for line in range(lines):
            high, low = rim[spare + line : spare + line + 1, :], rim[BAND + spare + line : BAND + spare + line + 1, :]
            wide_lines.append(high * 32.0 + low)
    if per % LANES == 0:
        landed = jnp.concatenate(wide_lines, 1).astype(jnp.int32)
        for s in range(shards):
            small_all[0:heads, s * per : (s + 1) * per] = small_in[s]
    else:
        total, landed = jnp.zeros((heads, rows), F32), jnp.zeros((1, rows), F32)
        for s in range(shards):
            spread = (iota((LANES, rows), 0) + s * per == iota((LANES, rows), 1)) & (iota((LANES, rows), 0) < per)
            spread = spread.astype(F32)
            total = total + dot(small_in[s], spread[0:per, :].astype(BF16))
            tall = jnp.broadcast_to(wide_lines[s], (8, LANES))
            landed = landed + jnp.dot(tall, spread, precision=HIGHEST, preferred_element_type=F32)[0:1, :]
        small_all[0:heads, :] = total.astype(BF16)
        landed = landed.astype(jnp.int32)

    def unsort_rows(b):
        unsort_ref[block_of(b), :] = one_hot(landed, b * BLOCK, BLOCK)

    each(0, chunks, unsort_rows)

    def convolve(value, j, taps_ref, col, out_ref):
        packed_ref[RIM:, :] = value
        for k in range(width - 1):
            packed_ref[RIM - (width - 1) + k : RIM - (width - 1) + k + 1, :] = rim_ref[pl.ds(k * BAND + j, 1), :]
        taps = taps_ref[:, col]
        total = taps[0:1, :] * packed_ref[RIM:, :]
        for lag in range(1, width):
            moved = taps[lag : lag + 1, :] * packed_ref[RIM - lag : RIM - lag + rows, :]
            total = total + jnp.where(avail_ref[...] >= lag, moved, 0.0)
        out_ref[:, col] = (total * jax.nn.sigmoid(total)).astype(BF16)

    def x_piece(j):
        col = pl.ds(pl.multiple_of(j * LANES, LANES), LANES)
        convolve(dot(unsort_ref[...], came[j]), j, conv_x_ref, col, x_ref)

    for pair in range(pairs, 2 * pairs):
        load(pair).wait()
    def project():
        for side in range(2):
            quarters = [bc_all[2 * r + side].reshape(shards, half, LANES) for r in range(peers // 2)]
            together = jnp.concatenate(quarters, 1).reshape(rows, LANES)
            value = dot(unsort_ref[...], together)
            here = slice(side * LANES, (side + 1) * LANES)
            if side == 0:
                convolve(value, pieces, conv_bc_ref, here, key_ref)
            else:
                convolve(value, pieces + 1, conv_bc_ref, here, query_ref)

    def common(chunk):
        origin = base + chunk * BLOCK
        here = block_of(chunk)
        column = iota((BLOCK, 1), 0) + origin
        document = doc_at(starts, column)
        raw = dot(unsort_ref[here, :], small_all[...], ((1,), (1,)))
        raw = raw + head_row(dt_bias_ref)[0:1, :]
        lane = iota((1, LANES), 1)
        step = jnp.maximum(raw, 0.0) + jnp.log1p(jnp.exp(-jnp.abs(raw)))
        step = jnp.where(lane < heads, step, 0.0)
        rate = jnp.exp(head_row(a_log_ref)[0:1, :])
        decay = -rate * step
        lower = iota((BLOCK, BLOCK), 0) >= iota((BLOCK, BLOCK), 1)
        sums = jnp.dot(lower.astype(F32), decay, precision=HIGHEST, preferred_element_type=F32)
        sums_ref[here, :] = sums
        sums_t_ref[chunk] = sums.T[0:heads, :]
        step_t_ref[chunk] = step.T[0:heads, :]
        document_row = doc_at(starts, iota((1, BLOCK), 1) + origin)
        linked = lower & (document == document_row)
        scores_ref[chunk] = jnp.where(
            linked, dot(query_ref[here, LANES:], key_ref[here, :], ((1,), (1,))), 0.0
        )
        before_doc = jnp.where(origin > 0, doc_at(starts, origin - 1), 0)
        base_doc = jnp.where(base > 0, doc_at(starts, base - 1), 0)
        last_doc = doc_at(starts, origin + BLOCK - 1)
        carried_ref[here, :] = jnp.where(document == before_doc, jnp.exp(sums), 0.0)
        last = sums[BLOCK - 1 : BLOCK, :]
        closing = jnp.where(document == last_doc, jnp.exp(jnp.minimum(last - sums, 0.0)), 0.0) * step
        closing_ref[here, :] = closing
        before = before_ref[0:1, :]
        carry_ref[here, :] = jnp.where(document == base_doc, jnp.exp(before + sums), 0.0)
        before_ref[...] = jnp.broadcast_to(before + last, before_ref.shape)

    def scan(group, chunk):
        cols = slice(group * span, (group + 1) * span)
        here = block_of(chunk)
        keys, query = key_ref[here, :], query_ref[here, LANES:]
        inside = inside_ref[:, cols]
        carried_all = expanded(carried_ref[here, :], inside)
        state = state_ref[:, cols]
        x32 = x_ref[here, cols].astype(F32)
        y_ref[here, cols] = carried_all * dot_right(query, state) + skip_ref[0:1, cols] * x32
        weighted = expanded(closing_ref[here, :], inside) * x32
        state_ref[:, cols] = carried_all[BLOCK - 1 : BLOCK, :] * state + dot_turned(keys, weighted)
        scores = scores_ref[chunk]
        for head in range(group * group_heads, (group + 1) * group_heads):
            first, end = head * head_dim, (head + 1) * head_dim
            low, high = first // LANES * LANES, -(-end // LANES) * LANES
            gap = sums_ref[here, head : head + 1] - sums_t_ref[chunk, head : head + 1, :]
            weight = jnp.exp(jnp.minimum(gap, 0.0)) * step_t_ref[chunk, head : head + 1, :] * scores
            channel = iota((1, high - low), 1) + low
            x_own = x_ref[here, low:high].astype(F32)
            x_own = jnp.where((channel >= first) & (channel < end), x_own, 0.0).astype(BF16)
            y_ref[here, low:high] += dot_left(weight, x_own)

    def chain(group):
        cols = slice(group * span, (group + 1) * span)

        @pl.when(me > 0)
        def _():
            state_copy(group).wait_recv()

        @pl.when(me < shards - 1)
        def _():
            keep = expanded(carry_ref[rows - 8 : rows, :], inside_ref[:, cols])[7:8, :]
            passed = state_ref[:, cols]
            incoming = jnp.where(me > 0, state_in[group].astype(F32), 0.0)
            state_out[group] = (keep * incoming + passed).astype(BF16)
            state_copy(group).start()

        @pl.when(me > 0)
        def _():
            def add(chunk):
                here = block_of(chunk)
                carried = expanded(carry_ref[here, :], inside_ref[:, cols])
                y_ref[here, cols] += carried * dot(query_ref[here, LANES:], state_in[group])

            each(0, chunks, add)

    def gate_piece(j):
        col = pl.ds(pl.multiple_of(j * LANES, LANES), LANES)

        for b in range(chunks):
            here = block_of(b)
            gate = dot(unsort_ref[here, :], came[pieces + j])
            gated = y_ref[here, col] * (gate * jax.nn.sigmoid(gate))
            y_ref[here, col] = gated * gain_line[0:1, col]
            square_ref[here, :] += gated * gated

    rim_total = rim_in[0].astype(F32)
    for s in range(1, shards):
        rim_total = rim_total + rim_in[s].astype(F32)
    rim_ref[...] = rim_total

    def early(q):
        @pl.when(q > 0)
        def _():
            pump(q)

        x_piece(q)

        @pl.when(q < 2)
        def _():
            pick(pairs + q)

        @pl.when(q == 1)
        def _():
            each(1, peers, lambda i: wide_copy(i).wait())
            project()

        @pl.when((q == 2) | (q == 3))
        def _():
            each((q - 2) * (chunks // 2), (q - 1) * (chunks // 2), common)

    each(0, group_pieces, early)

    turn = 2 * jnp.minimum(me, chunks - 1)
    first_turn = group_pieces + chunks - 1
    last_turn = pieces + 1
    open_turn = last_turn + 3

    def finished(q):
        count = 2 * (q - open_turn + 1) - jnp.where(q >= open_turn + 2, 1, 0)
        return jnp.clip(count, 0, pieces)

    def late(q):
        @pl.when(q <= first_turn)
        def _():
            scan(0, q - group_pieces)

        @pl.when(q == first_turn + turn)
        def _():
            chain(0)

        @pl.when(q == last_turn + turn)
        def _():
            chain(1)

        pump(q)

        @pl.when(q < pieces)
        def _():
            x_piece(q)

        @pl.when(q < group_pieces + pairs - 2)
        def _():
            pick(pairs + 2 + q - group_pieces)

        @pl.when((q == pieces - 1) | (q == pieces))
        def _():
            half_chunks = chunks // 2
            each((q - pieces + 1) * half_chunks, (q - pieces + 2) * half_chunks, lambda c: scan(1, c))

        each(finished(q - 1), finished(q), gate_piece)

    each(group_pieces, 2 * pieces, late)

    high, low = halves(square_ref[...])
    ones = jnp.ones((16, LANES), BF16)
    total = dot(ones, high, ((1,), (1,))) + dot(ones, low, ((1,), (1,)))
    squares[own] = jnp.concatenate([total[0:1, k : k + LANES] for k in range(0, rows, LANES)], 0)
    each(1, peers, lambda i: square_copy(i).start())

    def sent(q):
        each(1, shards, lambda i: piece_copy(q, i).wait_send())

    each(0, 2 * pieces, sent)

    @pl.when(me < shards - 1)
    def _():
        for group in range(GROUPS):
            state_copy(group).wait_send()

    each(1, peers, lambda i: square_copy(i).wait())
    total = squares[0]
    for peer in range(1, peers):
        total = total + squares[peer]
    total_ref[...] = total


def layer(lengths, a_log, dt_bias, d_skip, place, dt, conv_x, conv_bc, gain, xs, gate, bc):
    shards, peers = lax.axis_size("seq"), lax.axis_size("head")
    rows, inner = xs.shape
    heads = a_log.shape[0]
    per = rows // shards
    half = per // (peers // 2)
    chunks = rows // BLOCK
    pieces = inner // LANES
    wide = 2 * LANES
    span = inner // GROUPS
    vmem = pl.BlockSpec(memory_space=pltpu.VMEM)
    hbm = pl.BlockSpec(memory_space=pltpu.HBM)
    return pl.pallas_call(
        functools.partial(layer_kernel, heads),
        in_specs=[pl.BlockSpec(memory_space=pltpu.SMEM)] * 4 + [vmem] * 5 + [hbm] * 3,
        out_specs=[vmem, vmem],
        out_shape=[pltpu.VMEM((rows, inner), F32), pltpu.VMEM((rows // LANES, LANES), F32)],
        scratch_shapes=[
            pltpu.VMEM((pieces, rows, wide), BF16),
            pltpu.VMEM((rows, wide), BF16),
            pltpu.VMEM((rows, rows), BF16),
            pltpu.VMEM((rows, rows), BF16),
            pltpu.VMEM((2 * pieces, rows, LANES), BF16),
            pltpu.VMEM((2 * pieces, rows, LANES), BF16),
            pltpu.VMEM((shards, heads, per), BF16),
            pltpu.VMEM((shards, heads, per), BF16),
            pltpu.VMEM((LANES, rows), BF16),
            pltpu.VMEM((shards * half, LANES), BF16),
            pltpu.VMEM((peers, shards * half, LANES), BF16),
            pltpu.VMEM((shards, TAIL, LANES), F32),
            pltpu.VMEM((shards, TAIL, LANES), BF16),
            pltpu.VMEM((shards, TAIL, LANES), BF16),
            pltpu.VMEM((TAIL, LANES), F32),
            pltpu.VMEM((RIM + rows, LANES), F32),
            pltpu.VMEM((rows, LANES), jnp.int32),
            pltpu.VMEM((LANES, inner), BF16),
            pltpu.VMEM((rows, inner), BF16),
            pltpu.VMEM((rows, LANES), BF16),
            pltpu.VMEM((rows, wide), BF16),
            pltpu.VMEM((rows, LANES), F32),
            pltpu.VMEM((chunks, heads, BLOCK), F32),
            pltpu.VMEM((chunks, heads, BLOCK), F32),
            pltpu.VMEM((chunks, BLOCK, BLOCK), F32),
            pltpu.VMEM((rows, LANES), F32),
            pltpu.VMEM((rows, LANES), F32),
            pltpu.VMEM((rows, LANES), F32),
            pltpu.VMEM((8, LANES), F32),
            pltpu.VMEM((LANES, inner), F32),
            pltpu.VMEM((GROUPS, LANES, span), BF16),
            pltpu.VMEM((GROUPS, LANES, span), BF16),
            pltpu.VMEM((8, inner), F32),
            pltpu.VMEM((8, inner), F32),
            pltpu.VMEM((rows, LANES), F32),
            pltpu.VMEM((peers, rows // LANES, LANES), F32),
            pltpu.SemaphoreType.DMA((pieces + 1,)),
            pltpu.SemaphoreType.DMA((2, 2 * pieces, shards)),
            pltpu.SemaphoreType.DMA((2, shards)),
            pltpu.SemaphoreType.DMA((2, shards)),
            pltpu.SemaphoreType.DMA((2, shards)),
            pltpu.SemaphoreType.DMA((2, peers)),
            pltpu.SemaphoreType.DMA((2, GROUPS)),
            pltpu.SemaphoreType.DMA((2, peers)),
        ],
        compiler_params=pltpu.CompilerParams(
            collective_id=0, has_side_effects=True, vmem_limit_bytes=KERNEL_BYTES
        ),
    )(lengths, a_log, dt_bias, d_skip, place, dt, conv_x, conv_bc, gain, xs, gate, bc)


def scale_kernel(full_inner, y_ref, total_ref, out_hbm, out_ref, store_sems):
    blocks = y_ref.shape[0] // LANES

    def store(k):
        here = block_of(k, LANES)
        return pltpu.make_async_copy(out_ref.at[here], out_hbm.at[here], store_sems.at[k])

    scale = lax.rsqrt(total_ref[...] / full_inner + 1e-05)
    for k in range(blocks):
        here = block_of(k, LANES)
        column = jnp.broadcast_to(scale[k : k + 1, :], (LANES, LANES)).T[:, 0:1]
        out_ref[here, :] = (y_ref[here, :] * column).astype(BF16)
        store(k).start()
    for k in range(blocks):
        store(k).wait()


def scaled(y, total, full_inner):
    rows, inner = y.shape
    vmem = pl.BlockSpec(memory_space=pltpu.VMEM)
    return pl.pallas_call(
        functools.partial(scale_kernel, full_inner),
        in_specs=[vmem, vmem],
        out_specs=pl.BlockSpec(memory_space=pltpu.HBM),
        out_shape=jax.ShapeDtypeStruct((rows, inner), BF16),
        scratch_shapes=[
            pltpu.VMEM((rows, inner), BF16),
            pltpu.SemaphoreType.DMA((rows // LANES,)),
        ],
        compiler_params=pltpu.CompilerParams(vmem_limit_bytes=KERNEL_BYTES),
    )(
        pltpu.with_memory_space_constraint(y, pltpu.VMEM),
        pltpu.with_memory_space_constraint(total, pltpu.VMEM),
    )


def body(
    xs, gate_in, bc_in, dt_in, placement, lengths,
    conv_x, conv_bc, a_log, dt_bias, d_skip, norm_gain, *, full_inner,
):
    y, total = layer(
        lengths, a_log, dt_bias, d_skip, placement[None, :], dt_in.T, conv_x, conv_bc, norm_gain,
        xs, gate_in, bc_in,
    )
    return scaled(y, total, full_inner)


def solution(mesh):
    in_specs = (
        P(("parts", "seq"), "head"),
        P(("parts", "seq"), "head"),
        P(("parts", "seq"), None),
        P(("parts", "seq"), "head"),
        P(("parts", "seq")),
        P("parts"),
        P(None, "head"),
        P(),
        P("head"),
        P("head"),
        P("head"),
        P("head"),
    )
    out_specs = P(("parts", "seq"), "head")

    def whole(*args):
        step = functools.partial(body, full_inner=args[0].shape[1])
        return jax.shard_map(
            step, mesh=mesh, in_specs=in_specs, out_specs=out_specs, check_vma=False
        )(*args)

    return whole
```

```python
import functools

import jax
import jax.numpy as jnp
from jax import lax
from jax.experimental import pallas as pl
from jax.experimental.pallas import tpu as pltpu
from jax.sharding import PartitionSpec as P

BLOCK = 256
LANES = 128
RIM = 8
KERNEL_BYTES = 56800 << 10
GROUPS = 2
WINDOW = 2
BAND = 16
TAIL = 48
HIGHEST = lax.Precision.HIGHEST
MESH = pl.DeviceIdType.MESH
F32 = jnp.float32
BF16 = jnp.bfloat16


def iota(shape, dim):
    return lax.broadcasted_iota(jnp.int32, shape, dim)


def dot(a, b, dims=((1,), (0,))):
    return lax.dot_general(a, b, (dims, ((), ())), preferred_element_type=F32)


def halves(value):
    high = value.astype(BF16)
    return high, (value - high.astype(F32)).astype(BF16)


def dot_left(a, b):
    high, low = halves(a)
    return dot(high, b) + dot(low, b)


def dot_right(a, b):
    high, low = halves(b)
    return dot(jnp.concatenate([a, a], 1), jnp.concatenate([high, low], 0))


def dot_turned(a, b):
    high, low = halves(b)
    dims = ((0,), (0,))
    return dot(a, high, dims) + dot(a, low, dims)


def remote(source, target, sends, receives, axis, offset):
    count, me = lax.axis_size(axis), lax.axis_index(axis)
    return pltpu.make_async_remote_copy(
        src_ref=source,
        dst_ref=target,
        send_sem=sends,
        recv_sem=receives,
        device_id={axis: lax.rem(me + offset, count)},
        device_id_type=MESH,
    )


def each(first, last, action):
    def once(i, _):
        action(i)
        return 0

    lax.fori_loop(first, last, once, 0)


def doc_at(starts, position):
    total = jnp.where(starts[0] <= position, 1, 0)
    for start in starts[1:]:
        total = total + jnp.where(start <= position, 1, 0)
    return total


def starts_of(length_ref):
    starts = [jnp.int32(0)]
    for j in range(length_ref.shape[0] - 1):
        starts.append(starts[-1] + length_ref[j])
    return starts


def head_row(ref):
    lane = iota((8, LANES), 1)
    row = jnp.zeros((8, LANES), F32)
    for head in range(ref.shape[0]):
        row = jnp.where(lane == head, ref[head], row)
    return row


def expanded(value, inside):
    high, low = halves(value)
    low = pltpu.roll(low.astype(F32), LANES // 2, 1)
    lane = iota((1, LANES), 1)
    both = jnp.where(lane < LANES // 2, high.astype(F32), low)
    return dot(both.astype(BF16), inside)


def block_of(chunk, size=BLOCK):
    if isinstance(chunk, int):
        return pl.ds(chunk * size, size)
    return pl.ds(pl.multiple_of(chunk * size, size), size)


def one_hot(keys, first, count):
    return (iota((count, keys.shape[1]), 0) + first == keys).astype(F32).astype(BF16)


def slots_of(target, groups):
    rows = target.shape[1]
    chosen = (iota((groups, rows), 0) == target).astype(F32)
    before = (iota((LANES, LANES), 0) < iota((LANES, LANES), 1)).astype(F32).astype(BF16)
    blocks = [chosen[:, k : k + LANES] for k in range(0, rows, LANES)]
    inside = dot(jnp.concatenate(blocks, 0).astype(BF16), before)
    offset = jnp.zeros((groups, 1), F32)
    slots = []
    for k, block in enumerate(blocks):
        ranks = inside[k * groups : (k + 1) * groups, :] + offset
        slots.append(jnp.sum(block * ranks, axis=0, keepdims=True))
        offset = offset + jnp.sum(block, axis=1, keepdims=True)
    return jnp.concatenate(slots, 1).astype(jnp.int32)


def layer_kernel(
    heads, length_ref, a_log_ref, dt_bias_ref, d_skip_ref, place_ref, dt_ref, conv_x_ref, conv_bc_ref, gain_ref,
    x_hbm, gate_hbm, bc_hbm,
    y_ref, total_ref,
    given, bc_ref, sort_ref, unsort_ref, send, came, small_send, small_in, small_all,
    bc_send, bc_all, rim_rows, rim_send, rim_in, rim_ref, packed_ref, avail_ref, inside_ref,
    x_ref, key_ref, query_ref, sums_ref, sums_t_ref, step_t_ref, scores_ref,
    carried_ref, closing_ref, carry_ref, before_ref, state_ref, state_in, state_out, skip_ref, gain_line,
    square_ref, squares,
    load_sems, sems, small_sems, bc_sems, rim_sems, wide_sems, state_sems, square_sems,
):
    shards, peers = lax.axis_size("seq"), lax.axis_size("head")
    me, own = lax.axis_index("seq"), lax.axis_index("head")
    rows, inner = y_ref.shape
    per = rows // shards
    half = per // (peers // 2)
    head_dim = inner // heads
    chunks = rows // BLOCK
    pieces = inner // LANES
    wide = 2 * LANES
    pairs = pieces // 2
    width = conv_x_ref.shape[0]
    group_heads = heads // GROUPS
    span = inner // GROUPS
    group_pieces = pieces // GROUPS
    base = me * rows
    lanes = min(per, LANES)
    lines = per // lanes
    spare = pieces + 2
    mine = pl.ds(pl.multiple_of(me * per, per), per)
    starts = starts_of(length_ref)

    def load(pair):
        source = x_hbm if pair < pairs else gate_hbm
        first = (pair if pair < pairs else pair - pairs) * wide
        return pltpu.make_async_copy(source.at[:, first : first + wide], given.at[pair], load_sems.at[pair])

    bc_load = pltpu.make_async_copy(bc_hbm, bc_ref, load_sems.at[2 * pairs])

    def part(owner):
        return pl.ds(pl.multiple_of(owner * per, per), per)

    def piece_copy(q, i):
        return remote(
            send.at[q, part(lax.rem(me + i, shards))], came.at[q, mine],
            sems.at[0, q, i], sems.at[1, q, i], "seq", i,
        )

    def small_copy(i):
        return remote(
            small_send.at[lax.rem(me + i, shards)], small_in.at[me],
            small_sems.at[0, i], small_sems.at[1, i], "seq", i,
        )

    def bc_copy(i):
        dest = lax.rem(me + i, shards)
        return remote(
            bc_send.at[pl.ds(pl.multiple_of(dest * half, half), half)],
            bc_all.at[own, pl.ds(pl.multiple_of(me * half, half), half)],
            bc_sems.at[0, i], bc_sems.at[1, i], "seq", i,
        )

    def rim_copy(i):
        return remote(
            rim_send.at[lax.rem(me + i, shards)], rim_in.at[me],
            rim_sems.at[0, i], rim_sems.at[1, i], "seq", i,
        )

    def wide_copy(i):
        return remote(bc_all.at[own], bc_all.at[own], wide_sems.at[0, i], wide_sems.at[1, i], "head", i)

    def state_copy(group):
        return remote(
            state_out.at[group], state_in.at[group],
            state_sems.at[0, group], state_sems.at[1, group], "seq", 1,
        )

    def square_copy(i):
        return remote(
            squares.at[own], squares.at[own], square_sems.at[0, i], square_sems.at[1, i], "head", i
        )

    def start(q):
        each(1, shards, lambda i: piece_copy(q, i).start())

    def receive(q):
        each(1, shards, lambda i: piece_copy(q, i).wait_recv())

    barrier = pltpu.get_barrier_semaphore()
    for axis in ("seq", "head"):
        count, here = lax.axis_size(axis), lax.axis_index(axis)

        def signal(i, axis=axis, count=count, here=here):
            pl.semaphore_signal(
                barrier, inc=1, device_id={axis: lax.rem(here + i, count)}, device_id_type=MESH
            )

        each(1, count, signal)

    for pair in range(pairs):
        load(pair).start()
        if pair == 0:
            bc_load.start()

    place = place_ref[0:1, :]
    target = lax.shift_right_logical(place, rows.bit_length() - 1)
    local = place & (rows - 1)
    slot = slots_of(target, -(-shards // 16) * 16)
    key = target * per + slot

    def sort_rows(b):
        sort_ref[block_of(b), :] = one_hot(key, b * BLOCK, BLOCK)

    each(0, chunks, sort_rows)

    def pick(pair):
        def rows_of(b):
            value = dot(sort_ref[block_of(b), :], given[pair]).astype(BF16)
            send[2 * pair, block_of(b), :] = value[:, :LANES]
            send[2 * pair + 1, block_of(b), :] = value[:, LANES:]

        each(0, chunks, rows_of)
        for q in (2 * pair, 2 * pair + 1):
            came[q, mine, :] = send[q, mine, :]

    load(0).wait()
    pick(0)
    pl.semaphore_wait(barrier, shards - 1 + peers - 1)
    start(0)
    for pair in range(pairs, 2 * pairs):
        load(pair).start()

    rim_rows[...] = jnp.zeros_like(rim_rows)
    digits = jnp.where(iota((16, rows), 0) == 0, local >> 5, local & 31).astype(F32).astype(BF16)
    digits = jnp.concatenate([dt_ref[...], digits], 0)

    def small_rows(d):
        values = dot(digits, sort_ref[part(d), :], ((1,), (1,)))
        small_send[d] = values[0:heads, :].astype(BF16)
        for k in range(2):
            for line in range(lines):
                rim_rows[d, k * BAND + spare + line : k * BAND + spare + line + 1, 0:lanes] = values[
                    heads + k : heads + k + 1, line * lanes : (line + 1) * lanes
                ]

    each(0, shards, small_rows)
    small_in[me] = small_send[me]
    bc_load.wait()
    bc_cols = pl.ds(pl.multiple_of(lax.rem(own, 2) * LANES, LANES), LANES)
    bc_first = own // 2 * half

    def bc_rows(d):
        source = sort_ref[pl.ds(pl.multiple_of(d * per + bc_first, half), half), :]
        bc_send[pl.ds(pl.multiple_of(d * half, half), half), :] = dot(source, bc_ref[:, bc_cols]).astype(BF16)

    each(0, shards, bc_rows)
    bc_mine = pl.ds(pl.multiple_of(me * half, half), half)
    bc_all[own, bc_mine, :] = bc_send[bc_mine, :]

    each(1, shards, lambda i: small_copy(i).start())
    each(1, shards, lambda i: bc_copy(i).start())

    line = iota((RIM * shards, 1), 0)
    back = line & (RIM - 1)
    wanted = lax.shift_right_logical(line, RIM.bit_length() - 1) * rows - (width - 1) + back
    wanted = jnp.where((back < width - 1) & (wanted >= 0), wanted, -1)
    rim_pick = (wanted == place).astype(F32).astype(BF16)

    def rim_put(value, j):
        for d in range(shards):
            for k in range(width - 1):
                rim_rows[d, pl.ds(k * BAND + j, 1), :] = value[d * RIM + k : d * RIM + k + 1, :]

    def rim_of(value, j):
        rim_put(value[:, :LANES], j)
        rim_put(value[:, LANES:], j + 1)

    rim_of(dot(rim_pick, bc_ref[...]), pieces)
    for pair in range(1, pairs):
        load(pair).wait()
    each(0, pairs, lambda pair: rim_of(dot(rim_pick, given[pair]), 2 * pair))
    rim_send[...] = rim_rows[...].astype(BF16)
    rim_in[me] = rim_send[me]
    each(1, shards, lambda i: rim_copy(i).start())
    start(1)
    each(1, pairs, pick)

    for b in range(chunks):
        position = iota((BLOCK, 1), 0) + (base + b * BLOCK)
        first = jnp.zeros((BLOCK, 1), jnp.int32)
        for begin in starts[1:]:
            first = jnp.where(begin <= position, begin, first)
        avail_ref[b * BLOCK : (b + 1) * BLOCK, :] = jnp.broadcast_to(position - first, (BLOCK, LANES))
    head, channel = iota((LANES, inner), 0), iota((LANES, inner), 1)
    head = jnp.where(head < LANES // 2, head, head - LANES // 2)
    inside = (channel >= head * head_dim) & (channel < (head + 1) * head_dim)
    inside_ref[...] = inside.astype(F32).astype(BF16)
    gain_line[...] = jnp.broadcast_to(gain_ref[...].reshape(1, inner), gain_line.shape)
    skip_ref[...] = expanded(head_row(d_skip_ref), inside_ref[...])
    state_ref[...] = jnp.zeros_like(state_ref)
    before_ref[...] = jnp.zeros_like(before_ref)
    square_ref[...] = jnp.zeros_like(square_ref)
    small_all[...] = jnp.zeros_like(small_all)

    def ahead(q):
        return jnp.minimum(q + 1 + WINDOW + jnp.where(q >= 2 * pieces - 6, 2, 0), 2 * pieces)

    def pump(q):
        receive(q)
        each(jnp.where(q > 0, ahead(q - 1), WINDOW), ahead(q), start)

    pump(0)
    each(1, shards, lambda i: bc_copy(i).wait())
    each(1, peers, lambda i: wide_copy(i).start())
    each(1, shards, lambda i: small_copy(i).wait())
    each(1, shards, lambda i: rim_copy(i).wait())
    wide_lines = []
    for s in range(shards):
        rim = rim_in[s].astype(F32)
        for line in range(lines):
            high, low = rim[spare + line : spare + line + 1, :], rim[BAND + spare + line : BAND + spare + line + 1, :]
            wide_lines.append(high * 32.0 + low)
    if per % LANES == 0:
        landed = jnp.concatenate(wide_lines, 1).astype(jnp.int32)
        for s in range(shards):
            small_all[0:heads, s * per : (s + 1) * per] = small_in[s]
    else:
        total, landed = jnp.zeros((heads, rows), F32), jnp.zeros((1, rows), F32)
        for s in range(shards):
            spread = (iota((LANES, rows), 0) + s * per == iota((LANES, rows), 1)) & (iota((LANES, rows), 0) < per)
            spread = spread.astype(F32)
            total = total + dot(small_in[s], spread[0:per, :].astype(BF16))
            tall = jnp.broadcast_to(wide_lines[s], (8, LANES))
            landed = landed + jnp.dot(tall, spread, precision=HIGHEST, preferred_element_type=F32)[0:1, :]
        small_all[0:heads, :] = total.astype(BF16)
        landed = landed.astype(jnp.int32)

    def unsort_rows(b):
        unsort_ref[block_of(b), :] = one_hot(landed, b * BLOCK, BLOCK)

    each(0, chunks, unsort_rows)

    def convolve(value, j, taps_ref, col, out_ref):
        packed_ref[RIM:, :] = value
        for k in range(width - 1):
            packed_ref[RIM - (width - 1) + k : RIM - (width - 1) + k + 1, :] = rim_ref[pl.ds(k * BAND + j, 1), :]
        taps = taps_ref[:, col]
        total = taps[0:1, :] * packed_ref[RIM:, :]
        for lag in range(1, width):
            moved = taps[lag : lag + 1, :] * packed_ref[RIM - lag : RIM - lag + rows, :]
            total = total + jnp.where(avail_ref[...] >= lag, moved, 0.0)
        out_ref[:, col] = (total * jax.nn.sigmoid(total)).astype(BF16)

    def x_piece(j):
        col = pl.ds(pl.multiple_of(j * LANES, LANES), LANES)
        convolve(dot(unsort_ref[...], came[j]), j, conv_x_ref, col, x_ref)

    for pair in range(pairs, 2 * pairs):
        load(pair).wait()
    def project():
        for side in range(2):
            quarters = [bc_all[2 * r + side].reshape(shards, half, LANES) for r in range(peers // 2)]
            together = jnp.concatenate(quarters, 1).reshape(rows, LANES)
            value = dot(unsort_ref[...], together)
            here = slice(side * LANES, (side + 1) * LANES)
            if side == 0:
                convolve(value, pieces, conv_bc_ref, here, key_ref)
            else:
                convolve(value, pieces + 1, conv_bc_ref, here, query_ref)

    def common(chunk):
        origin = base + chunk * BLOCK
        here = block_of(chunk)
        column = iota((BLOCK, 1), 0) + origin
        document = doc_at(starts, column)
        raw = dot(unsort_ref[here, :], small_all[...], ((1,), (1,)))
        raw = raw + head_row(dt_bias_ref)[0:1, :]
        lane = iota((1, LANES), 1)
        step = jnp.maximum(raw, 0.0) + jnp.log1p(jnp.exp(-jnp.abs(raw)))
        step = jnp.where(lane < heads, step, 0.0)
        rate = jnp.exp(head_row(a_log_ref)[0:1, :])
        decay = -rate * step
        lower = iota((BLOCK, BLOCK), 0) >= iota((BLOCK, BLOCK), 1)
        sums = jnp.dot(lower.astype(F32), decay, precision=HIGHEST, preferred_element_type=F32)
        sums_ref[here, :] = sums
        sums_t_ref[chunk] = sums.T[0:heads, :]
        step_t_ref[chunk] = step.T[0:heads, :]
        document_row = doc_at(starts, iota((1, BLOCK), 1) + origin)
        linked = lower & (document == document_row)
        scores_ref[chunk] = jnp.where(
            linked, dot(query_ref[here, LANES:], key_ref[here, :], ((1,), (1,))), 0.0
        )
        before_doc = jnp.where(origin > 0, doc_at(starts, origin - 1), 0)
        base_doc = jnp.where(base > 0, doc_at(starts, base - 1), 0)
        last_doc = doc_at(starts, origin + BLOCK - 1)
        carried_ref[here, :] = jnp.where(document == before_doc, jnp.exp(sums), 0.0)
        last = sums[BLOCK - 1 : BLOCK, :]
        closing = jnp.where(document == last_doc, jnp.exp(jnp.minimum(last - sums, 0.0)), 0.0) * step
        closing_ref[here, :] = closing
        before = before_ref[0:1, :]
        carry_ref[here, :] = jnp.where(document == base_doc, jnp.exp(before + sums), 0.0)
        before_ref[...] = jnp.broadcast_to(before + last, before_ref.shape)

    def scan(group, chunk):
        cols = slice(group * span, (group + 1) * span)
        here = block_of(chunk)
        keys, query = key_ref[here, :], query_ref[here, LANES:]
        inside = inside_ref[:, cols]
        carried_all = expanded(carried_ref[here, :], inside)
        state = state_ref[:, cols]
        x32 = x_ref[here, cols].astype(F32)
        y_ref[here, cols] = carried_all * dot_right(query, state) + skip_ref[0:1, cols] * x32
        weighted = expanded(closing_ref[here, :], inside) * x32
        state_ref[:, cols] = carried_all[BLOCK - 1 : BLOCK, :] * state + dot_turned(keys, weighted)
        scores = scores_ref[chunk]
        for head in range(group * group_heads, (group + 1) * group_heads):
            first, end = head * head_dim, (head + 1) * head_dim
            low, high = first // LANES * LANES, -(-end // LANES) * LANES
            gap = sums_ref[here, head : head + 1] - sums_t_ref[chunk, head : head + 1, :]
            weight = jnp.exp(jnp.minimum(gap, 0.0)) * step_t_ref[chunk, head : head + 1, :] * scores
            channel = iota((1, high - low), 1) + low
            x_own = x_ref[here, low:high].astype(F32)
            x_own = jnp.where((channel >= first) & (channel < end), x_own, 0.0).astype(BF16)
            y_ref[here, low:high] += dot_left(weight, x_own)

    def chain(group):
        cols = slice(group * span, (group + 1) * span)

        @pl.when(me > 0)
        def _():
            state_copy(group).wait_recv()

        @pl.when(me < shards - 1)
        def _():
            keep = expanded(carry_ref[rows - 8 : rows, :], inside_ref[:, cols])[7:8, :]
            passed = state_ref[:, cols]
            incoming = jnp.where(me > 0, state_in[group].astype(F32), 0.0)
            state_out[group] = (keep * incoming + passed).astype(BF16)
            state_copy(group).start()

        @pl.when(me > 0)
        def _():
            def add(chunk):
                here = block_of(chunk)
                carried = expanded(carry_ref[here, :], inside_ref[:, cols])
                y_ref[here, cols] += carried * dot(query_ref[here, LANES:], state_in[group])

            each(0, chunks, add)

    def gate_piece(j):
        col = pl.ds(pl.multiple_of(j * LANES, LANES), LANES)

        for b in range(chunks):
            here = block_of(b)
            gate = dot(unsort_ref[here, :], came[pieces + j])
            gated = y_ref[here, col] * (gate * jax.nn.sigmoid(gate))
            y_ref[here, col] = gated * gain_line[0:1, col]
            square_ref[here, :] += gated * gated

    rim_total = rim_in[0].astype(F32)
    for s in range(1, shards):
        rim_total = rim_total + rim_in[s].astype(F32)
    rim_ref[...] = rim_total

    def early(q):
        @pl.when(q > 0)
        def _():
            pump(q)

        x_piece(q)

        @pl.when(q < 2)
        def _():
            pick(pairs + q)

        @pl.when(q == 1)
        def _():
            each(1, peers, lambda i: wide_copy(i).wait())
            project()

        @pl.when((q == 2) | (q == 3))
        def _():
            each((q - 2) * (chunks // 2), (q - 1) * (chunks // 2), common)

    each(0, group_pieces, early)

    turn = 2 * jnp.minimum(me, chunks - 1)
    first_turn = group_pieces + chunks - 1
    last_turn = pieces + 1
    open_turn = last_turn + 3

    def finished(q):
        count = 2 * (q - open_turn + 1) - jnp.where(q >= open_turn + 2, 1, 0)
        return jnp.clip(count, 0, pieces)

    def late(q):
        @pl.when(q <= first_turn)
        def _():
            scan(0, q - group_pieces)

        @pl.when(q == first_turn + turn)
        def _():
            chain(0)

        @pl.when(q == last_turn + turn)
        def _():
            chain(1)

        pump(q)

        @pl.when(q < pieces)
        def _():
            x_piece(q)

        @pl.when(q < group_pieces + pairs - 2)
        def _():
            pick(pairs + 2 + q - group_pieces)

        @pl.when((q == pieces - 1) | (q == pieces))
        def _():
            half_chunks = chunks // 2
            each((q - pieces + 1) * half_chunks, (q - pieces + 2) * half_chunks, lambda c: scan(1, c))

        each(finished(q - 1), finished(q), gate_piece)

    each(group_pieces, 2 * pieces, late)

    high, low = halves(square_ref[...])
    ones = jnp.ones((16, LANES), BF16)
    total = dot(ones, high, ((1,), (1,))) + dot(ones, low, ((1,), (1,)))
    squares[own] = jnp.concatenate([total[0:1, k : k + LANES] for k in range(0, rows, LANES)], 0)
    each(1, peers, lambda i: square_copy(i).start())

    def sent(q):
        each(1, shards, lambda i: piece_copy(q, i).wait_send())

    each(0, 2 * pieces, sent)

    @pl.when(me < shards - 1)
    def _():
        for group in range(GROUPS):
            state_copy(group).wait_send()

    each(1, peers, lambda i: square_copy(i).wait())
    total = squares[0]
    for peer in range(1, peers):
        total = total + squares[peer]
    total_ref[...] = total


def layer(lengths, a_log, dt_bias, d_skip, place, dt, conv_x, conv_bc, gain, xs, gate, bc):
    shards, peers = lax.axis_size("seq"), lax.axis_size("head")
    rows, inner = xs.shape
    heads = a_log.shape[0]
    per = rows // shards
    half = per // (peers // 2)
    chunks = rows // BLOCK
    pieces = inner // LANES
    wide = 2 * LANES
    span = inner // GROUPS
    vmem = pl.BlockSpec(memory_space=pltpu.VMEM)
    hbm = pl.BlockSpec(memory_space=pltpu.HBM)
    return pl.pallas_call(
        functools.partial(layer_kernel, heads),
        in_specs=[pl.BlockSpec(memory_space=pltpu.SMEM)] * 4 + [vmem] * 5 + [hbm] * 3,
        out_specs=[vmem, vmem],
        out_shape=[pltpu.VMEM((rows, inner), F32), pltpu.VMEM((rows // LANES, LANES), F32)],
        scratch_shapes=[
            pltpu.VMEM((pieces, rows, wide), BF16),
            pltpu.VMEM((rows, wide), BF16),
            pltpu.VMEM((rows, rows), BF16),
            pltpu.VMEM((rows, rows), BF16),
            pltpu.VMEM((2 * pieces, rows, LANES), BF16),
            pltpu.VMEM((2 * pieces, rows, LANES), BF16),
            pltpu.VMEM((shards, heads, per), BF16),
            pltpu.VMEM((shards, heads, per), BF16),
            pltpu.VMEM((LANES, rows), BF16),
            pltpu.VMEM((shards * half, LANES), BF16),
            pltpu.VMEM((peers, shards * half, LANES), BF16),
            pltpu.VMEM((shards, TAIL, LANES), F32),
            pltpu.VMEM((shards, TAIL, LANES), BF16),
            pltpu.VMEM((shards, TAIL, LANES), BF16),
            pltpu.VMEM((TAIL, LANES), F32),
            pltpu.VMEM((RIM + rows, LANES), F32),
            pltpu.VMEM((rows, LANES), jnp.int32),
            pltpu.VMEM((LANES, inner), BF16),
            pltpu.VMEM((rows, inner), BF16),
            pltpu.VMEM((rows, LANES), BF16),
            pltpu.VMEM((rows, wide), BF16),
            pltpu.VMEM((rows, LANES), F32),
            pltpu.VMEM((chunks, heads, BLOCK), F32),
            pltpu.VMEM((chunks, heads, BLOCK), F32),
            pltpu.VMEM((chunks, BLOCK, BLOCK), F32),
            pltpu.VMEM((rows, LANES), F32),
            pltpu.VMEM((rows, LANES), F32),
            pltpu.VMEM((rows, LANES), F32),
            pltpu.VMEM((8, LANES), F32),
            pltpu.VMEM((LANES, inner), F32),
            pltpu.VMEM((GROUPS, LANES, span), BF16),
            pltpu.VMEM((GROUPS, LANES, span), BF16),
            pltpu.VMEM((8, inner), F32),
            pltpu.VMEM((8, inner), F32),
            pltpu.VMEM((rows, LANES), F32),
            pltpu.VMEM((peers, rows // LANES, LANES), F32),
            pltpu.SemaphoreType.DMA((pieces + 1,)),
            pltpu.SemaphoreType.DMA((2, 2 * pieces, shards)),
            pltpu.SemaphoreType.DMA((2, shards)),
            pltpu.SemaphoreType.DMA((2, shards)),
            pltpu.SemaphoreType.DMA((2, shards)),
            pltpu.SemaphoreType.DMA((2, peers)),
            pltpu.SemaphoreType.DMA((2, GROUPS)),
            pltpu.SemaphoreType.DMA((2, peers)),
        ],
        compiler_params=pltpu.CompilerParams(
            collective_id=0, has_side_effects=True, vmem_limit_bytes=KERNEL_BYTES
        ),
    )(lengths, a_log, dt_bias, d_skip, place, dt, conv_x, conv_bc, gain, xs, gate, bc)


def scale_kernel(full_inner, y_ref, total_ref, out_hbm, out_ref, store_sems):
    blocks = y_ref.shape[0] // LANES

    def store(k):
        here = block_of(k, LANES)
        return pltpu.make_async_copy(out_ref.at[here], out_hbm.at[here], store_sems.at[k])

    scale = lax.rsqrt(total_ref[...] / full_inner + 1e-05)
    for k in range(blocks):
        here = block_of(k, LANES)
        column = jnp.broadcast_to(scale[k : k + 1, :], (LANES, LANES)).T[:, 0:1]
        out_ref[here, :] = (y_ref[here, :] * column).astype(BF16)
        store(k).start()
    for k in range(blocks):
        store(k).wait()


def scaled(y, total, full_inner):
    rows, inner = y.shape
    vmem = pl.BlockSpec(memory_space=pltpu.VMEM)
    return pl.pallas_call(
        functools.partial(scale_kernel, full_inner),
        in_specs=[vmem, vmem],
        out_specs=pl.BlockSpec(memory_space=pltpu.HBM),
        out_shape=jax.ShapeDtypeStruct((rows, inner), BF16),
        scratch_shapes=[
            pltpu.VMEM((rows, inner), BF16),
            pltpu.SemaphoreType.DMA((rows // LANES,)),
        ],
        compiler_params=pltpu.CompilerParams(vmem_limit_bytes=KERNEL_BYTES),
    )(
        pltpu.with_memory_space_constraint(y, pltpu.VMEM),
        pltpu.with_memory_space_constraint(total, pltpu.VMEM),
    )


def body(
    xs, gate_in, bc_in, dt_in, placement, lengths,
    conv_x, conv_bc, a_log, dt_bias, d_skip, norm_gain, *, full_inner,
):
    y, total = layer(
        lengths, a_log, dt_bias, d_skip, placement[None, :], dt_in.T, conv_x, conv_bc, norm_gain,
        xs, gate_in, bc_in,
    )
    return scaled(y, total, full_inner)


def solution(mesh):
    in_specs = (
        P(("parts", "seq"), "head"),
        P(("parts", "seq"), "head"),
        P(("parts", "seq"), None),
        P(("parts", "seq"), "head"),
        P(("parts", "seq")),
        P("parts"),
        P(None, "head"),
        P(),
        P("head"),
        P("head"),
        P("head"),
        P("head"),
    )
    out_specs = P(("parts", "seq"), "head")

    def whole(*args):
        step = functools.partial(body, full_inner=args[0].shape[1])
        return jax.shard_map(
            step, mesh=mesh, in_specs=in_specs, out_specs=out_specs, check_vma=False
        )(*args)

    return whole
```
